32 devices in a mesh: ha: 8 (over y, x, core), wa: 4 (over z).
Axes of the slice: x: 2, y: 2, z: 4, core: 2. Of those that a mesh axis runs over, the one named last changes fastest.
Arguments:
- row_features: bfloat16 [64, 256, 256], P('ha', 'wa'), may hold values from -24 to 24
- row_table_query: bfloat16 [511, 64], replicated, may hold values from -3 to 3
- row_table_value: bfloat16 [511, 128], replicated, may hold values from -3 to 3
- column_query_key: bfloat16 [64, 256, 128], P(None, ('ha', 'wa')), may hold values from -24 to 24
- column_table_query: bfloat16 [127, 64], replicated, may hold values from -3 to 3
- column_table_value: bfloat16 [127, 128], replicated, may hold values from -3 to 3
- output_cotangent: bfloat16 [64, 256, 128], P(None, ('ha', 'wa')), may hold values from -6 to 6
Outputs:
- row_feature_gradient: bfloat16 [64, 256, 256], P('ha', 'wa')
- column_query_key_gradient: bfloat16 [64, 256, 128], P(None, ('ha', 'wa'))
- row_table_query_gradient: float32 [511, 64], P(None, 'wa')
- row_table_value_gradient: float32 [511, 128], P(None, 'wa')
- column_table_query_gradient: float32 [127, 64], P(None, 'wa')
- column_table_value_gradient: float32 [127, 128], P(None, 'wa')
The draws below stay inside these ranges and needn't reach their ends.
All inputs are finite; a program needn't handle non-finite values.
Results may differ from the reference program's by a relative error of at most 0.015.
Values may be sent and summed in bfloat16 or wider, within the bound.
A program may use at most 128 MiB of HBM per device.

```python
import math
import jax
import jax.numpy as jnp
from jax import lax

HEAD_COUNT = 4
KEY_SIZE = 16
VALUE_SIZE = 32
HEIGHT = 64
WIDTH = 256
ROW_TABLE = 511
COLUMN_TABLE = 127


def line_draws(base_key, pass_tag, line_count, length):
    seed_list = [jax.random.fold_in(base_key, pass_tag * 32 + number) for number in range(12)]
    table_length = 2 * length - 1
    table_query = jnp.clip(0.5 * jax.random.normal(seed_list[0], (table_length, HEAD_COUNT, KEY_SIZE), jnp.float32), -3.0, 3.0)
    shape_full = (line_count, length, HEAD_COUNT, KEY_SIZE)
    shape_scale = (line_count, length, 1, 1)
    queries = jax.random.normal(seed_list[1], shape_full, jnp.float32)
    key_vectors = jax.random.normal(seed_list[2], shape_full, jnp.float32)
    queries = queries * jnp.exp(jax.random.uniform(seed_list[3], shape_scale, jnp.float32, math.log(0.5), math.log(1.5)))
    key_vectors = key_vectors * jnp.exp(jax.random.uniform(seed_list[4], shape_scale, jnp.float32, math.log(0.3), math.log(3.0)))
    return (jnp.clip(queries, -24.0, 24.0), jnp.clip(key_vectors, -24.0, 24.0), table_query)


def draw_row_features(key, part):
    queries, key_vectors, unused = line_draws(key, 1, HEIGHT, WIDTH)
    value_seed = jax.random.fold_in(key, 977)
    values = jnp.clip(jax.random.normal(value_seed, (HEIGHT, WIDTH, HEAD_COUNT * VALUE_SIZE), jnp.float32), -6.0, 6.0)
    joined = jnp.concatenate([queries.reshape(HEIGHT, WIDTH, HEAD_COUNT * KEY_SIZE), key_vectors.reshape(HEIGHT, WIDTH, HEAD_COUNT * KEY_SIZE), values], axis=-1)
    return joined.astype(jnp.bfloat16)


def draw_row_table_query(key, part):
    table_query = line_draws(key, 1, HEIGHT, WIDTH)[2]
    return table_query.reshape(ROW_TABLE, HEAD_COUNT * KEY_SIZE).astype(jnp.bfloat16)


def draw_column_query_key(key, part):
    queries, key_vectors, unused = line_draws(key, 2, WIDTH, HEIGHT)
    joined = jnp.concatenate([queries.reshape(WIDTH, HEIGHT, HEAD_COUNT * KEY_SIZE), key_vectors.reshape(WIDTH, HEIGHT, HEAD_COUNT * KEY_SIZE)], axis=-1)
    return jnp.swapaxes(joined, 0, 1).astype(jnp.bfloat16)


def draw_column_table_query(key, part):
    table_query = line_draws(key, 2, WIDTH, HEIGHT)[2]
    return table_query.reshape(COLUMN_TABLE, HEAD_COUNT * KEY_SIZE).astype(jnp.bfloat16)


def level_of(rng, extent, shards, smallest, largest):
    def one(position, parts):
        heights = jax.random.uniform(jax.random.fold_in(jax.random.fold_in(rng, 6), position), (parts,), jnp.float32, smallest / len(shards), largest / len(shards))
        return jnp.repeat(jnp.exp(heights), extent[position] // parts).reshape((-1,) + (1,) * (len(extent) - position - 1))

    gain = one(*shards[0])
    for cut in shards[1:]:
        gain = gain * one(*cut)
    return gain


def centred(stream_key, shape, scale, limit, cuts=(), kind=jnp.bfloat16):
    factor_of = level_of(stream_key, shape, cuts, -0.22, 0.18) if cuts else 1.0
    result = jax.random.normal(stream_key, shape, jnp.float32) * scale * factor_of
    return jnp.minimum(jnp.maximum(result, -limit), limit).astype(kind)


def setup_inputs(seed: int = 0) -> dict:
    arg_keys = jax.random.split(jax.random.key(seed), 8)
    return {
        "row_features": draw_row_features(jax.random.fold_in(arg_keys[7], 71), 0),
        "row_table_query": draw_row_table_query(jax.random.fold_in(arg_keys[7], 71), 0),
        "row_table_value": centred(arg_keys[2], (ROW_TABLE, HEAD_COUNT * VALUE_SIZE), 0.5, 3.0),
        "column_query_key": draw_column_query_key(jax.random.fold_in(arg_keys[7], 71), 0),
        "column_table_query": draw_column_table_query(jax.random.fold_in(arg_keys[7], 71), 0),
        "column_table_value": centred(arg_keys[5], (COLUMN_TABLE, HEAD_COUNT * VALUE_SIZE), 0.5, 3.0),
        "output_cotangent": centred(arg_keys[6], (HEIGHT, WIDTH, HEAD_COUNT * VALUE_SIZE), 1.0, 6.0, ((1, 32),)),
    }


def to_absolute(table_scores):
    length = table_scores.shape[-2]
    query_place = jnp.arange(length)[:, None]
    key_place = jnp.arange(length)[None, :]
    offsets = (key_place - query_place + length - 1).astype(jnp.int32)
    offsets = jnp.broadcast_to(offsets, table_scores.shape[:-1] + (length,))
    return jnp.take_along_axis(table_scores, offsets, axis=-1)


def to_relative(square):
    length = square.shape[-1]
    table_length = 2 * length - 1
    query_place = jnp.arange(length)[:, None]
    offset_place = jnp.arange(table_length)[None, :]
    source = offset_place + query_place - length + 1
    inside = (source >= 0) & (source < length)
    clipped = jnp.clip(source, 0, length - 1).astype(jnp.int32)
    clipped = jnp.broadcast_to(clipped, square.shape[:-1] + (table_length,))
    picked = jnp.take_along_axis(square, clipped, axis=-1)
    return jnp.where(inside, picked, jnp.zeros((), square.dtype))


def line_probabilities(queries, key_vectors, table_query, logit_scale):
    direct = jnp.einsum("ohd,phd->hop", queries.astype(jnp.float32), key_vectors.astype(jnp.float32))
    table_part = jnp.einsum("ohd,rhd->hor", queries.astype(jnp.float32), table_query.astype(jnp.float32))
    return jax.nn.softmax(logit_scale * (direct + to_absolute(table_part)), axis=-1)


def line_forward(queries, key_vectors, values, table_query, table_value, logit_scale):
    probabilities = line_probabilities(queries, key_vectors, table_query, logit_scale)
    weights = probabilities.astype(jnp.bfloat16)
    mixture = jnp.einsum("hop,phd->ohd", weights.astype(jnp.float32), values.astype(jnp.float32))
    mixture = mixture + jnp.einsum("hor,rhd->ohd", to_relative(weights).astype(jnp.float32), table_value.astype(jnp.float32))
    return mixture.astype(jnp.bfloat16)


def line_backward(queries, key_vectors, values, table_query, table_value, upstream, logit_scale):
    probabilities = line_probabilities(queries, key_vectors, table_query, logit_scale)
    weights = probabilities.astype(jnp.bfloat16)
    upstream_wide = upstream.astype(jnp.float32)
    weight_grad = jnp.einsum("ohd,phd->hop", upstream_wide, values.astype(jnp.float32))
    weight_grad = weight_grad + to_absolute(jnp.einsum("ohd,rhd->hor", upstream_wide, table_value.astype(jnp.float32)))
    score_grad = probabilities * (weight_grad - jnp.sum(probabilities * weight_grad, axis=-1, keepdims=True))
    score_grad = score_grad.astype(jnp.bfloat16)
    score_table = to_relative(score_grad).astype(jnp.float32)
    weight_table = to_relative(weights).astype(jnp.float32)
    score_wide = score_grad.astype(jnp.float32)
    query_wide = queries.astype(jnp.float32)
    query_grad = jnp.einsum("hop,phd->ohd", score_wide, key_vectors.astype(jnp.float32))
    query_grad = query_grad + jnp.einsum("hor,rhd->ohd", score_table, table_query.astype(jnp.float32))
    query_grad = (logit_scale * query_grad).astype(jnp.bfloat16)
    key_grad = (logit_scale * jnp.einsum("hop,ohd->phd", score_wide, query_wide)).astype(jnp.bfloat16)
    value_grad = jnp.einsum("hop,ohd->phd", weights.astype(jnp.float32), upstream_wide).astype(jnp.bfloat16)
    table_query_grad = logit_scale * jnp.einsum("hor,ohd->rhd", score_table, query_wide)
    table_value_grad = jnp.einsum("hor,ohd->rhd", weight_table, upstream_wide)
    return query_grad, key_grad, value_grad, table_query_grad, table_value_grad


def reference(row_features, row_table_query, row_table_value, column_query_key, column_table_query, column_table_value, output_cotangent):
    query_width = HEAD_COUNT * KEY_SIZE
    value_width = HEAD_COUNT * VALUE_SIZE
    logit_scale = KEY_SIZE ** -0.5
    row_queries = row_features[:, :, :query_width].reshape(HEIGHT, WIDTH, HEAD_COUNT, KEY_SIZE)
    row_keys = row_features[:, :, query_width:2 * query_width].reshape(HEIGHT, WIDTH, HEAD_COUNT, KEY_SIZE)
    row_values = row_features[:, :, 2 * query_width:].reshape(HEIGHT, WIDTH, HEAD_COUNT, VALUE_SIZE)
    row_query_table = row_table_query.reshape(ROW_TABLE, HEAD_COUNT, KEY_SIZE)
    row_value_table = row_table_value.reshape(ROW_TABLE, HEAD_COUNT, VALUE_SIZE)
    column_query_table = column_table_query.reshape(COLUMN_TABLE, HEAD_COUNT, KEY_SIZE)
    column_value_table = column_table_value.reshape(COLUMN_TABLE, HEAD_COUNT, VALUE_SIZE)

    row_output = lax.map(
        lambda triple: line_forward(triple[0], triple[1], triple[2], row_query_table, row_value_table, logit_scale),
        (row_queries, row_keys, row_values))

    column_queries = jnp.swapaxes(column_query_key[:, :, :query_width], 0, 1).reshape(WIDTH, HEIGHT, HEAD_COUNT, KEY_SIZE)
    column_keys = jnp.swapaxes(column_query_key[:, :, query_width:], 0, 1).reshape(WIDTH, HEIGHT, HEAD_COUNT, KEY_SIZE)
    column_values = jnp.swapaxes(row_output, 0, 1)
    column_upstream = jnp.swapaxes(output_cotangent, 0, 1).reshape(WIDTH, HEIGHT, HEAD_COUNT, VALUE_SIZE)

    def column_step(totals, line_inputs):
        gradients = line_backward(line_inputs[0], line_inputs[1], line_inputs[2], column_query_table, column_value_table, line_inputs[3], logit_scale)
        return (totals[0] + gradients[3], totals[1] + gradients[4]), (gradients[0], gradients[1], gradients[2])

    column_start = (jnp.zeros((COLUMN_TABLE, HEAD_COUNT, KEY_SIZE), jnp.float32), jnp.zeros((COLUMN_TABLE, HEAD_COUNT, VALUE_SIZE), jnp.float32))
    column_totals, column_grads = lax.scan(column_step, column_start, (column_queries, column_keys, column_values, column_upstream))
    row_upstream = jnp.swapaxes(column_grads[2], 0, 1)

    def row_step(totals, line_inputs):
        gradients = line_backward(line_inputs[0], line_inputs[1], line_inputs[2], row_query_table, row_value_table, line_inputs[3], logit_scale)
        return (totals[0] + gradients[3], totals[1] + gradients[4]), (gradients[0], gradients[1], gradients[2])

    row_start = (jnp.zeros((ROW_TABLE, HEAD_COUNT, KEY_SIZE), jnp.float32), jnp.zeros((ROW_TABLE, HEAD_COUNT, VALUE_SIZE), jnp.float32))
    row_totals, row_grads = lax.scan(row_step, row_start, (row_queries, row_keys, row_values, row_upstream))

    row_feature_gradient = jnp.concatenate([
        row_grads[0].reshape(HEIGHT, WIDTH, query_width),
        row_grads[1].reshape(HEIGHT, WIDTH, query_width),
        row_grads[2].reshape(HEIGHT, WIDTH, value_width)], axis=-1)
    column_query_key_gradient = jnp.swapaxes(jnp.concatenate([
        column_grads[0].reshape(WIDTH, HEIGHT, query_width),
        column_grads[1].reshape(WIDTH, HEIGHT, query_width)], axis=-1), 0, 1)
    return (row_feature_gradient, column_query_key_gradient,
            row_totals[0].reshape(ROW_TABLE, query_width), row_totals[1].reshape(ROW_TABLE, value_width),
            column_totals[0].reshape(COLUMN_TABLE, query_width), column_totals[1].reshape(COLUMN_TABLE, value_width))
```

```python
import functools

import jax
import jax.numpy as jnp
from jax import lax
from jax.experimental import pallas as pl
from jax.experimental.pallas import tpu as pltpu
from jax.sharding import PartitionSpec as P

HEAD_COUNT = 4
KEY_SIZE = 16
VALUE_SIZE = 32
QUERY_WIDTH = HEAD_COUNT * KEY_SIZE
VALUE_WIDTH = HEAD_COUNT * VALUE_SIZE
LOGIT_SCALE = KEY_SIZE ** (-0.5)
F32 = jnp.float32
BF16 = jnp.bfloat16


def dot(a, b):
    return lax.dot_general(a, b, (((1,), (0,)), ((), ())), preferred_element_type=F32)


def dot_t(a, b):
    return lax.dot_general(a, b, (((1,), (1,)), ((), ())), preferred_element_type=F32)


def flip_matrix(length, block):
    i = lax.broadcasted_iota(jnp.int32, (length, length), 0)
    j = lax.broadcasted_iota(jnp.int32, (length, length), 1)
    same = (i // block == j // block) & (i % block + j % block == block - 1)
    return jnp.where(same, 1.0, 0.0).astype(BF16)


def head_mask(head, width, per_head):
    lane = lax.broadcasted_iota(jnp.int32, (1, width), 1)
    return jnp.where(lane // per_head == head, 1.0, 0.0).astype(BF16)


def head_rows_mask(length, width, per_head):
    shape = (HEAD_COUNT * length, width)
    row = lax.broadcasted_iota(jnp.int32, shape, 0)
    lane = lax.broadcasted_iota(jnp.int32, shape, 1)
    return jnp.where(lane // per_head == row // length, 1.0, 0.0).astype(BF16)


def to_absolute(table):
    length = table.shape[0]
    return pltpu.roll(table, length + 1, 1, stride=1, stride_axis=0)[:, :length]


def to_relative(flipped):
    padded = jnp.concatenate([flipped, jnp.zeros_like(flipped)], axis=1)
    return pltpu.roll(padded, 0, 1, stride=1, stride_axis=0)


def softmax(logits):
    e = jnp.exp(logits - jnp.max(logits, axis=1, keepdims=True))
    return e * (1.0 / jnp.sum(e, axis=1, keepdims=True))


def row_forward(x_ref, rq_ref, rv_ref, out_ref, p_ref, w_ref):
    lines, length, _ = x_ref.shape
    flip = flip_matrix(length, length)

    def line(n, carry):
        x = x_ref[n]
        q, k, v = x[:, :QUERY_WIDTH], x[:, QUERY_WIDTH : 2 * QUERY_WIDTH], x[:, 2 * QUERY_WIDTH :]
        kr = jnp.concatenate([rq_ref[...], k], axis=0)
        vs = jnp.concatenate([rv_ref[...], v], axis=0)
        out = jnp.zeros((length, VALUE_WIDTH), F32)
        for h in range(HEAD_COUNT):
            s = dot_t(q * head_mask(h, QUERY_WIDTH, KEY_SIZE), kr)
            p = softmax(
                LOGIT_SCALE * (s[:, 2 * length :] + to_absolute(s[:, : 2 * length]))
            )
            p_ref[n, h] = p
            flipped = dot(flip, p.astype(BF16))
            both = jnp.concatenate([to_relative(flipped), flipped], axis=1).astype(BF16)
            w_ref[n, h] = both
            out = out + dot(both, vs * head_mask(h, VALUE_WIDTH, VALUE_SIZE))
        out_ref[n] = dot(flip, out.astype(BF16)).astype(BF16)
        return carry

    lax.fori_loop(0, lines, line, 0)


def row_backward(x_ref, d_ref, p_ref, w_ref, rq_ref, rv_ref, gx_ref, tq_ref, tv_ref):
    lines, length, _ = x_ref.shape
    flip = flip_matrix(length, length)
    tq_ref[...] = jnp.zeros_like(tq_ref)
    tv_ref[...] = jnp.zeros_like(tv_ref)

    def line(n, carry):
        x = x_ref[n]
        d = d_ref[n]
        q, k, v = x[:, :QUERY_WIDTH], x[:, QUERY_WIDTH : 2 * QUERY_WIDTH], x[:, 2 * QUERY_WIDTH :]
        kr = jnp.concatenate([rq_ref[...], k], axis=0)
        vs = jnp.concatenate([rv_ref[...], v], axis=0)
        qt = dot(flip, q).T.astype(BF16)
        dt = dot(flip, d).T.astype(BF16)
        qg = jnp.zeros((length, QUERY_WIDTH), F32)
        kg, vg = [], []
        for h in range(HEAD_COUNT):
            g = dot_t(d * head_mask(h, VALUE_WIDTH, VALUE_SIZE), vs)
            g = g[:, 2 * length :] + to_absolute(g[:, : 2 * length])
            p = p_ref[n, h]
            e = p * (g - jnp.sum(p * g, axis=1, keepdims=True))
            flipped = dot(flip, e.astype(BF16))
            both = jnp.concatenate([to_relative(flipped), flipped], axis=1).astype(BF16)
            qg = qg + dot(both, kr * head_mask(h, QUERY_WIDTH, KEY_SIZE))
            qs = slice(h * KEY_SIZE, (h + 1) * KEY_SIZE)
            t = LOGIT_SCALE * dot(qt[qs], both)
            tq_ref[qs] += t[:, : 2 * length]
            kg.append(t[:, 2 * length :])
            ds = slice(h * VALUE_SIZE, (h + 1) * VALUE_SIZE)
            u = dot(dt[ds], w_ref[n, h])
            tv_ref[ds] += u[:, : 2 * length]
            vg.append(u[:, 2 * length :])
        qg = dot(flip, (LOGIT_SCALE * qg).astype(BF16))
        kg = jnp.concatenate(kg, axis=0).T
        vg = jnp.concatenate(vg, axis=0).T
        gx_ref[n] = jnp.concatenate([qg, kg, vg], axis=1).astype(BF16)
        return carry

    lax.fori_loop(0, lines, line, 0)


def column_pass(qk_ref, u_ref, g_ref, rq_ref, rv_ref, gqk_ref, du_ref, tq_ref, tv_ref):
    columns, length, _ = qk_ref.shape
    rows = HEAD_COUNT * length
    flip_all = flip_matrix(rows, length)
    flip = flip_matrix(length, length)
    qmask = head_rows_mask(length, QUERY_WIDTH, KEY_SIZE)
    vmask = head_rows_mask(length, VALUE_WIDTH, VALUE_SIZE)
    tq_ref[...] = jnp.zeros_like(tq_ref)
    tv_ref[...] = jnp.zeros_like(tv_ref)

    def heads(x):
        return [x[h * length : (h + 1) * length] for h in range(HEAD_COUNT)]

    def absolute(s):
        shifted = [to_absolute(x) for x in heads(s[:, : 2 * length])]
        return s[:, 2 * length :] + jnp.concatenate(shifted, axis=0)

    def relative(flipped):
        shifted = [to_relative(x) for x in heads(flipped)]
        return jnp.concatenate([jnp.concatenate(shifted, axis=0), flipped], axis=1).astype(BF16)

    def column(c, carry):
        q, k = qk_ref[c, :, :QUERY_WIDTH], qk_ref[c, :, QUERY_WIDTH:]
        kr = jnp.concatenate([rq_ref[...], k], axis=0)
        us = jnp.concatenate([rv_ref[...], u_ref[c]], axis=0)
        qs = jnp.concatenate([q] * HEAD_COUNT, axis=0) * qmask
        gs = jnp.concatenate([g_ref[c]] * HEAD_COUNT, axis=0) * vmask
        p = softmax(LOGIT_SCALE * absolute(dot_t(qs, kr)))
        g = absolute(dot_t(gs, us))
        e = p * (g - jnp.sum(p * g, axis=1, keepdims=True))
        e = relative(dot(flip_all, e.astype(BF16)))
        w = relative(dot(flip_all, p.astype(BF16)))
        parts = heads(dot(e, kr))
        qg = jnp.zeros((length, QUERY_WIDTH), F32)
        for h in range(HEAD_COUNT):
            qg = qg + parts[h] * head_mask(h, QUERY_WIDTH, KEY_SIZE).astype(F32)
        qg = dot(flip, (LOGIT_SCALE * qg).astype(BF16))
        qt = dot(flip_all, qs).T.astype(BF16)
        gt = dot(flip_all, gs).T.astype(BF16)
        t = LOGIT_SCALE * dot(qt, e)
        tq_ref[...] += t[:, : 2 * length]
        gqk_ref[c] = jnp.concatenate([qg, t[:, 2 * length :].T], axis=1).astype(BF16)
        t = dot(gt, w)
        tv_ref[...] += t[:, : 2 * length]
        du_ref[c] = t[:, 2 * length :].T.astype(BF16)
        return carry

    lax.fori_loop(0, columns, column, 0)


def call(body, name, out_shapes, *operands):
    return pl.pallas_call(
        body,
        name=name,
        out_shape=[jax.ShapeDtypeStruct(s, t) for s, t in out_shapes],
        in_specs=[pl.BlockSpec(memory_space=pltpu.VMEM)] * len(operands),
        out_specs=[pl.BlockSpec(memory_space=pltpu.VMEM)] * len(out_shapes),
        compiler_params=pltpu.CompilerParams(vmem_limit_bytes=48 * 1024 * 1024),
    )(*operands)


def on_device(
    row_features,
    row_table_query,
    row_table_value,
    column_query_key,
    column_table_query,
    column_table_value,
    output_cotangent,
):
    both = ("ha", "wa")
    pad = lambda t: jnp.pad(t, ((0, 1), (0, 0)))
    row_tables = (pad(row_table_query), pad(row_table_value))
    column_tables = (pad(column_table_query), pad(column_table_value))
    row_lines = lax.all_to_all(row_features, "wa", split_axis=0, concat_axis=1, tiled=True)
    lines, length, channels = row_lines.shape
    row_output, probabilities, weights = call(
        row_forward,
        "row_forward",
        [
            ((lines, length, VALUE_WIDTH), BF16),
            ((lines, HEAD_COUNT, length, length), F32),
            ((lines, HEAD_COUNT, length, 3 * length), BF16),
        ],
        row_lines,
        *row_tables,
    )
    column_values = lax.all_to_all(row_output, both, split_axis=1, concat_axis=0, tiled=True)
    height, columns, _ = column_values.shape
    query_key_gradient, output_grad, column_sum_query, column_sum_value = call(
        column_pass,
        "column_pass",
        [
            ((columns, height, 2 * QUERY_WIDTH), BF16),
            ((columns, height, VALUE_WIDTH), BF16),
            ((QUERY_WIDTH, 2 * height), F32),
            ((VALUE_WIDTH, 2 * height), F32),
        ],
        column_query_key.swapaxes(0, 1),
        column_values.swapaxes(0, 1),
        output_cotangent.swapaxes(0, 1),
        *column_tables,
    )
    row_upstream = lax.all_to_all(
        output_grad.swapaxes(0, 1), both, split_axis=0, concat_axis=1, tiled=True
    )
    row_grad, row_sum_query, row_sum_value = call(
        row_backward,
        "row_backward",
        [
            ((lines, length, channels), BF16),
            ((QUERY_WIDTH, 2 * length), F32),
            ((VALUE_WIDTH, 2 * length), F32),
        ],
        row_lines,
        row_upstream,
        probabilities,
        weights,
        *row_tables,
    )
    row_feature_gradient = lax.all_to_all(row_grad, "wa", split_axis=1, concat_axis=0, tiled=True)
    groups = lax.axis_size("wa")
    sums = (row_sum_query, row_sum_value, column_sum_query, column_sum_value)
    joined = jnp.concatenate([s.astype(BF16).reshape(groups, -1) for s in sums], axis=1)
    share = lax.psum_scatter(joined, "wa", scatter_dimension=0, tiled=False)
    total = lax.psum(share, "ha").astype(F32)
    tables, start = [], 0
    for s in sums:
        size = s.size // groups
        table = total[start : start + size].reshape(s.shape[0] // groups, s.shape[1])
        tables.append(table[:, : s.shape[1] - 1].T)
        start += size
    return (row_feature_gradient, query_key_gradient.swapaxes(0, 1), *tables)


def solution(mesh):
    placed = (
        P("ha", "wa", None),
        P(),
        P(),
        P(None, ("ha", "wa"), None),
        P(),
        P(),
        P(None, ("ha", "wa"), None),
    )
    return jax.shard_map(
        on_device,
        mesh=mesh,
        in_specs=placed,
        out_specs=(
            P("ha", "wa", None),
            P(None, ("ha", "wa"), None),
            P(None, "wa"),
            P(None, "wa"),
            P(None, "wa"),
            P(None, "wa"),
        ),
        check_vma=False,
    )
```

```python
import functools

import jax
import jax.numpy as jnp
from jax import lax
from jax.experimental import pallas as pl
from jax.experimental.pallas import tpu as pltpu
from jax.sharding import PartitionSpec as P

HEAD_COUNT = 4
KEY_SIZE = 16
VALUE_SIZE = 32
QUERY_WIDTH = HEAD_COUNT * KEY_SIZE
VALUE_WIDTH = HEAD_COUNT * VALUE_SIZE
LOGIT_SCALE = KEY_SIZE ** (-0.5)
F32 = jnp.float32
BF16 = jnp.bfloat16


def dot(a, b):
    return lax.dot_general(a, b, (((1,), (0,)), ((), ())), preferred_element_type=F32)


def dot_t(a, b):
    return lax.dot_general(a, b, (((1,), (1,)), ((), ())), preferred_element_type=F32)


def flip_matrix(length, block):
    i = lax.broadcasted_iota(jnp.int32, (length, length), 0)
    j = lax.broadcasted_iota(jnp.int32, (length, length), 1)
    same = (i // block == j // block) & (i % block + j % block == block - 1)
    return jnp.where(same, 1.0, 0.0).astype(BF16)


def head_mask(head, width, per_head):
    lane = lax.broadcasted_iota(jnp.int32, (1, width), 1)
    return jnp.where(lane // per_head == head, 1.0, 0.0).astype(BF16)


def head_rows_mask(length, width, per_head):
    shape = (HEAD_COUNT * length, width)
    row = lax.broadcasted_iota(jnp.int32, shape, 0)
    lane = lax.broadcasted_iota(jnp.int32, shape, 1)
    return jnp.where(lane // per_head == row // length, 1.0, 0.0).astype(BF16)


def to_absolute(table):
    length = table.shape[0]
    return pltpu.roll(table, length + 1, 1, stride=1, stride_axis=0)[:, :length]


def to_relative(flipped):
    padded = jnp.concatenate([flipped, jnp.zeros_like(flipped)], axis=1)
    return pltpu.roll(padded, 0, 1, stride=1, stride_axis=0)


def softmax(logits):
    e = jnp.exp(logits - jnp.max(logits, axis=1, keepdims=True))
    return e * (1.0 / jnp.sum(e, axis=1, keepdims=True))


def row_forward(x_ref, rq_ref, rv_ref, out_ref, p_ref, w_ref):
    lines, length, _ = x_ref.shape
    flip = flip_matrix(length, length)

    def line(n, carry):
        x = x_ref[n]
        q, k, v = x[:, :QUERY_WIDTH], x[:, QUERY_WIDTH : 2 * QUERY_WIDTH], x[:, 2 * QUERY_WIDTH :]
        kr = jnp.concatenate([rq_ref[...], k], axis=0)
        vs = jnp.concatenate([rv_ref[...], v], axis=0)
        out = jnp.zeros((length, VALUE_WIDTH), F32)
        for h in range(HEAD_COUNT):
            s = dot_t(q * head_mask(h, QUERY_WIDTH, KEY_SIZE), kr)
            p = softmax(
                LOGIT_SCALE * (s[:, 2 * length :] + to_absolute(s[:, : 2 * length]))
            )
            p_ref[n, h] = p
            flipped = dot(flip, p.astype(BF16))
            both = jnp.concatenate([to_relative(flipped), flipped], axis=1).astype(BF16)
            w_ref[n, h] = both
            out = out + dot(both, vs * head_mask(h, VALUE_WIDTH, VALUE_SIZE))
        out_ref[n] = dot(flip, out.astype(BF16)).astype(BF16)
        return carry

    lax.fori_loop(0, lines, line, 0)


def row_backward(x_ref, d_ref, p_ref, w_ref, rq_ref, rv_ref, gx_ref, tq_ref, tv_ref):
    lines, length, _ = x_ref.shape
    flip = flip_matrix(length, length)
    tq_ref[...] = jnp.zeros_like(tq_ref)
    tv_ref[...] = jnp.zeros_like(tv_ref)

    def line(n, carry):
        x = x_ref[n]
        d = d_ref[n]
        q, k, v = x[:, :QUERY_WIDTH], x[:, QUERY_WIDTH : 2 * QUERY_WIDTH], x[:, 2 * QUERY_WIDTH :]
        kr = jnp.concatenate([rq_ref[...], k], axis=0)
        vs = jnp.concatenate([rv_ref[...], v], axis=0)
        qt = dot(flip, q).T.astype(BF16)
        dt = dot(flip, d).T.astype(BF16)
        qg = jnp.zeros((length, QUERY_WIDTH), F32)
        kg, vg = [], []
        for h in range(HEAD_COUNT):
            g = dot_t(d * head_mask(h, VALUE_WIDTH, VALUE_SIZE), vs)
            g = g[:, 2 * length :] + to_absolute(g[:, : 2 * length])
            p = p_ref[n, h]
            e = p * (g - jnp.sum(p * g, axis=1, keepdims=True))
            flipped = dot(flip, e.astype(BF16))
            both = jnp.concatenate([to_relative(flipped), flipped], axis=1).astype(BF16)
            qg = qg + dot(both, kr * head_mask(h, QUERY_WIDTH, KEY_SIZE))
            qs = slice(h * KEY_SIZE, (h + 1) * KEY_SIZE)
            t = LOGIT_SCALE * dot(qt[qs], both)
            tq_ref[qs] += t[:, : 2 * length]
            kg.append(t[:, 2 * length :])
            ds = slice(h * VALUE_SIZE, (h + 1) * VALUE_SIZE)
            u = dot(dt[ds], w_ref[n, h])
            tv_ref[ds] += u[:, : 2 * length]
            vg.append(u[:, 2 * length :])
        qg = dot(flip, (LOGIT_SCALE * qg).astype(BF16))
        kg = jnp.concatenate(kg, axis=0).T
        vg = jnp.concatenate(vg, axis=0).T
        gx_ref[n] = jnp.concatenate([qg, kg, vg], axis=1).astype(BF16)
        return carry

    lax.fori_loop(0, lines, line, 0)


def column_pass(qk_ref, u_ref, g_ref, rq_ref, rv_ref, gqk_ref, du_ref, tq_ref, tv_ref):
    columns, length, _ = qk_ref.shape
    rows = HEAD_COUNT * length
    flip_all = flip_matrix(rows, length)
    flip = flip_matrix(length, length)
    qmask = head_rows_mask(length, QUERY_WIDTH, KEY_SIZE)
    vmask = head_rows_mask(length, VALUE_WIDTH, VALUE_SIZE)
    tq_ref[...] = jnp.zeros_like(tq_ref)
    tv_ref[...] = jnp.zeros_like(tv_ref)

    def heads(x):
        return [x[h * length : (h + 1) * length] for h in range(HEAD_COUNT)]

    def absolute(s):
        shifted = [to_absolute(x) for x in heads(s[:, : 2 * length])]
        return s[:, 2 * length :] + jnp.concatenate(shifted, axis=0)

    def relative(flipped):
        shifted = [to_relative(x) for x in heads(flipped)]
        return jnp.concatenate([jnp.concatenate(shifted, axis=0), flipped], axis=1).astype(BF16)

    def column(c, carry):
        q, k = qk_ref[c, :, :QUERY_WIDTH], qk_ref[c, :, QUERY_WIDTH:]
        kr = jnp.concatenate([rq_ref[...], k], axis=0)
        us = jnp.concatenate([rv_ref[...], u_ref[c]], axis=0)
        qs = jnp.concatenate([q] * HEAD_COUNT, axis=0) * qmask
        gs = jnp.concatenate([g_ref[c]] * HEAD_COUNT, axis=0) * vmask
        p = softmax(LOGIT_SCALE * absolute(dot_t(qs, kr)))
        g = absolute(dot_t(gs, us))
        e = p * (g - jnp.sum(p * g, axis=1, keepdims=True))
        e = relative(dot(flip_all, e.astype(BF16)))
        w = relative(dot(flip_all, p.astype(BF16)))
        parts = heads(dot(e, kr))
        qg = jnp.zeros((length, QUERY_WIDTH), F32)
        for h in range(HEAD_COUNT):
            qg = qg + parts[h] * head_mask(h, QUERY_WIDTH, KEY_SIZE).astype(F32)
        qg = dot(flip, (LOGIT_SCALE * qg).astype(BF16))
        qt = dot(flip_all, qs).T.astype(BF16)
        gt = dot(flip_all, gs).T.astype(BF16)
        t = LOGIT_SCALE * dot(qt, e)
        tq_ref[...] += t[:, : 2 * length]
        gqk_ref[c] = jnp.concatenate([qg, t[:, 2 * length :].T], axis=1).astype(BF16)
        t = dot(gt, w)
        tv_ref[...] += t[:, : 2 * length]
        du_ref[c] = t[:, 2 * length :].T.astype(BF16)
        return carry

    lax.fori_loop(0, columns, column, 0)


def peer_id(index, sizes):
    ha_size, wa_size = sizes
    return {"ha": index // wa_size, "wa": index % wa_size}


def greet(me, count, to_id):
    barrier = pltpu.get_barrier_semaphore()

    def signal(k, carry):
        pl.semaphore_signal(
            barrier,
            inc=1,
            device_id=to_id(lax.rem(me + k, count)),
            device_id_type=pl.DeviceIdType.MESH,
        )
        return carry

    lax.fori_loop(1, count, signal, 0)
    pl.semaphore_wait(barrier, count - 1)


def swap_all(me, count, to_id, source, target, send_sems, recv_sems):
    def copy(peer, slot):
        return pltpu.make_async_remote_copy(
            src_ref=source(peer),
            dst_ref=target(slot),
            send_sem=send_sems.at[peer],
            recv_sem=recv_sems.at[slot],
            device_id=to_id(peer),
            device_id_type=pl.DeviceIdType.MESH,
        )

    def start(k, carry):
        copy(lax.rem(me + k, count), me).start()
        return carry

    def finish(k, carry):
        peer = lax.rem(me + k, count)
        copy(peer, peer).wait_recv()
        copy(peer, peer).wait_send()
        return carry

    lax.fori_loop(1, count, start, 0)
    return lambda: lax.fori_loop(1, count, finish, 0)


def table_kernel(sizes, x_ref, out_ref, got, send_sems, recv_sems, share_send, share_recv):
    ha_size, wa_size = sizes
    count = ha_size * wa_size
    ha, wa = lax.axis_index("ha"), lax.axis_index("wa")
    me = ha * wa_size + wa
    to_id = lambda i: peer_id(i, sizes)
    greet(me, count, to_id)
    finish = swap_all(
        me,
        count,
        to_id,
        lambda i: x_ref.at[i % wa_size, i // wa_size],
        lambda i: got.at[i],
        send_sems,
        recv_sems,
    )
    got[me] = x_ref[wa, ha]
    finish()
    total = lax.fori_loop(
        0, count, lambda i, t: t + got[i].astype(F32), jnp.zeros(got.shape[1:], F32)
    )
    out_ref[ha] = total
    finish = swap_all(
        ha,
        ha_size,
        lambda i: {"ha": i, "wa": wa},
        lambda i: out_ref.at[ha],
        lambda i: out_ref.at[i],
        share_send,
        share_recv,
    )
    finish()


def sum_tables(joined):
    sizes = (lax.axis_size("ha"), lax.axis_size("wa"))
    count = sizes[0] * sizes[1]
    return pl.pallas_call(
        functools.partial(table_kernel, sizes),
        name="sum_tables",
        out_shape=jax.ShapeDtypeStruct(joined.shape[1:], F32),
        in_specs=[pl.BlockSpec(memory_space=pltpu.VMEM)],
        out_specs=pl.BlockSpec(memory_space=pltpu.VMEM),
        scratch_shapes=[
            pltpu.VMEM((count, *joined.shape[2:]), BF16),
            pltpu.SemaphoreType.DMA((count,)),
            pltpu.SemaphoreType.DMA((count,)),
            pltpu.SemaphoreType.DMA((sizes[0],)),
            pltpu.SemaphoreType.DMA((sizes[0],)),
        ],
        compiler_params=pltpu.CompilerParams(collective_id=0, has_side_effects=True),
    )(joined)


def call(body, name, out_shapes, *operands):
    return pl.pallas_call(
        body,
        name=name,
        out_shape=[jax.ShapeDtypeStruct(s, t) for s, t in out_shapes],
        in_specs=[pl.BlockSpec(memory_space=pltpu.VMEM)] * len(operands),
        out_specs=[pl.BlockSpec(memory_space=pltpu.VMEM)] * len(out_shapes),
        compiler_params=pltpu.CompilerParams(vmem_limit_bytes=48 * 1024 * 1024),
    )(*operands)


def on_device(
    row_features,
    row_table_query,
    row_table_value,
    column_query_key,
    column_table_query,
    column_table_value,
    output_cotangent,
):
    both = ("ha", "wa")
    pad = lambda t: jnp.pad(t, ((0, 1), (0, 0)))
    row_tables = (pad(row_table_query), pad(row_table_value))
    column_tables = (pad(column_table_query), pad(column_table_value))
    row_lines = lax.all_to_all(row_features, "wa", split_axis=0, concat_axis=1, tiled=True)
    lines, length, channels = row_lines.shape
    row_output, probabilities, weights = call(
        row_forward,
        "row_forward",
        [
            ((lines, length, VALUE_WIDTH), BF16),
            ((lines, HEAD_COUNT, length, length), F32),
            ((lines, HEAD_COUNT, length, 3 * length), BF16),
        ],
        row_lines,
        *row_tables,
    )
    column_values = lax.all_to_all(row_output, both, split_axis=1, concat_axis=0, tiled=True)
    height, columns, _ = column_values.shape
    query_key_gradient, output_grad, column_sum_query, column_sum_value = call(
        column_pass,
        "column_pass",
        [
            ((columns, height, 2 * QUERY_WIDTH), BF16),
            ((columns, height, VALUE_WIDTH), BF16),
            ((QUERY_WIDTH, 2 * height), F32),
            ((VALUE_WIDTH, 2 * height), F32),
        ],
        column_query_key.swapaxes(0, 1),
        column_values.swapaxes(0, 1),
        output_cotangent.swapaxes(0, 1),
        *column_tables,
    )
    row_upstream = lax.all_to_all(
        output_grad.swapaxes(0, 1), both, split_axis=0, concat_axis=1, tiled=True
    )
    row_grad, row_sum_query, row_sum_value = call(
        row_backward,
        "row_backward",
        [
            ((lines, length, channels), BF16),
            ((QUERY_WIDTH, 2 * length), F32),
            ((VALUE_WIDTH, 2 * length), F32),
        ],
        row_lines,
        row_upstream,
        probabilities,
        weights,
        *row_tables,
    )
    row_feature_gradient = lax.all_to_all(row_grad, "wa", split_axis=1, concat_axis=0, tiled=True)
    groups = lax.axis_size("wa")
    sums = (row_sum_query, row_sum_value, column_sum_query, column_sum_value)
    joined = jnp.concatenate([s.astype(BF16).reshape(groups, -1) for s in sums], axis=1)
    height_groups = lax.axis_size("ha")
    joined = jnp.pad(joined, ((0, 0), (0, -joined.shape[1] % (height_groups * 128))))
    total = sum_tables(joined.reshape(groups, height_groups, -1, 128)).reshape(-1)
    tables, start = [], 0
    for s in sums:
        size = s.size // groups
        table = total[start : start + size].reshape(s.shape[0] // groups, s.shape[1])
        tables.append(table[:, : s.shape[1] - 1].T)
        start += size
    return (row_feature_gradient, query_key_gradient.swapaxes(0, 1), *tables)


def solution(mesh):
    placed = (
        P("ha", "wa", None),
        P(),
        P(),
        P(None, ("ha", "wa"), None),
        P(),
        P(),
        P(None, ("ha", "wa"), None),
    )
    return jax.shard_map(
        on_device,
        mesh=mesh,
        in_specs=placed,
        out_specs=(
            P("ha", "wa", None),
            P(None, ("ha", "wa"), None),
            P(None, "wa"),
            P(None, "wa"),
            P(None, "wa"),
            P(None, "wa"),
        ),
        check_vma=False,
    )
```

```python
import functools

import jax
import jax.numpy as jnp
from jax import lax
from jax.experimental import pallas as pl
from jax.experimental.pallas import tpu as pltpu
from jax.sharding import PartitionSpec as P

HEAD_COUNT = 4
KEY_SIZE = 16
VALUE_SIZE = 32
QUERY_WIDTH = HEAD_COUNT * KEY_SIZE
VALUE_WIDTH = HEAD_COUNT * VALUE_SIZE
LOGIT_SCALE = KEY_SIZE ** (-0.5)
F32 = jnp.float32
BF16 = jnp.bfloat16
SUBLANES = 8
LANES = 128


def dot(a, b):
    return lax.dot_general(a, b, (((1,), (0,)), ((), ())), preferred_element_type=F32)


def dot_t(a, b):
    return lax.dot_general(a, b, (((1,), (1,)), ((), ())), preferred_element_type=F32)


def flip_matrix(length, block):
    i = lax.broadcasted_iota(jnp.int32, (length, length), 0)
    j = lax.broadcasted_iota(jnp.int32, (length, length), 1)
    same = (i // block == j // block) & (i % block + j % block == block - 1)
    return jnp.where(same, 1.0, 0.0).astype(BF16)


def head_mask(head, width, per_head):
    lane = lax.broadcasted_iota(jnp.int32, (1, width), 1)
    return jnp.where(lane // per_head == head, 1.0, 0.0).astype(BF16)


def head_rows_mask(length, width, per_head):
    shape = (HEAD_COUNT * length, width)
    row = lax.broadcasted_iota(jnp.int32, shape, 0)
    lane = lax.broadcasted_iota(jnp.int32, shape, 1)
    return jnp.where(lane // per_head == row // length, 1.0, 0.0).astype(BF16)


def to_absolute(table):
    length = table.shape[0]
    return pltpu.roll(table, length + 1, 1, stride=1, stride_axis=0)[:, :length]


def to_relative(flipped):
    padded = jnp.concatenate([flipped, jnp.zeros_like(flipped)], axis=1)
    return pltpu.roll(padded, 0, 1, stride=1, stride_axis=0)


def softmax(logits):
    e = jnp.exp(logits - jnp.max(logits, axis=1, keepdims=True))
    return e * (1.0 / jnp.sum(e, axis=1, keepdims=True))


def row_forward(x_ref, rq_ref, rv_ref, out_ref, p_ref, w_ref):
    lines = x_ref.shape[1]
    length = p_ref.shape[2]
    columns = length // out_ref.shape[0]
    flip = flip_matrix(length, length)

    def line(n, carry):
        x = jnp.concatenate([x_ref[i, n] for i in range(x_ref.shape[0])], axis=0)
        q, k, v = x[:, :QUERY_WIDTH], x[:, QUERY_WIDTH : 2 * QUERY_WIDTH], x[:, 2 * QUERY_WIDTH :]
        kr = jnp.concatenate([rq_ref[...], k], axis=0)
        vs = jnp.concatenate([rv_ref[...], v], axis=0)
        out = jnp.zeros((length, VALUE_WIDTH), F32)
        for h in range(HEAD_COUNT):
            s = dot_t(q * head_mask(h, QUERY_WIDTH, KEY_SIZE), kr)
            p = softmax(
                LOGIT_SCALE * (s[:, 2 * length :] + to_absolute(s[:, : 2 * length]))
            )
            p_ref[n, h] = p
            flipped = dot(flip, p.astype(BF16))
            both = jnp.concatenate([to_relative(flipped), flipped], axis=1).astype(BF16)
            w_ref[n, h] = both
            out = out + dot(both, vs * head_mask(h, VALUE_WIDTH, VALUE_SIZE))
        out = dot(flip, out.astype(BF16))
        for i in range(out_ref.shape[0]):
            out_ref[i, n, :columns] = out[i * columns : (i + 1) * columns]
        return carry

    lax.fori_loop(0, lines, line, 0)


def row_backward(x_ref, d_ref, p_ref, w_ref, rq_ref, rv_ref, gx_ref, tq_ref, tv_ref, send):
    lines = x_ref.shape[1]
    length = p_ref.shape[2]
    columns = length // d_ref.shape[0]
    tile = gx_ref.shape[2]
    flip = flip_matrix(length, length)
    tq_ref[...] = jnp.zeros_like(tq_ref)
    tv_ref[...] = jnp.zeros_like(tv_ref)

    def line(n, carry):
        x = jnp.concatenate([x_ref[i, n] for i in range(x_ref.shape[0])], axis=0)
        d = jnp.concatenate([d_ref[i, n, :columns] for i in range(d_ref.shape[0])], axis=0)
        d = d.astype(BF16)
        q, k, v = x[:, :QUERY_WIDTH], x[:, QUERY_WIDTH : 2 * QUERY_WIDTH], x[:, 2 * QUERY_WIDTH :]
        kr = jnp.concatenate([rq_ref[...], k], axis=0)
        vs = jnp.concatenate([rv_ref[...], v], axis=0)
        qt = dot(flip, q).T.astype(BF16)
        dt = dot(flip, d).T.astype(BF16)
        qg = jnp.zeros((length, QUERY_WIDTH), F32)
        kg, vg = [], []
        for h in range(HEAD_COUNT):
            g = dot_t(d * head_mask(h, VALUE_WIDTH, VALUE_SIZE), vs)
            g = g[:, 2 * length :] + to_absolute(g[:, : 2 * length])
            p = p_ref[n, h]
            e = p * (g - jnp.sum(p * g, axis=1, keepdims=True))
            flipped = dot(flip, e.astype(BF16))
            both = jnp.concatenate([to_relative(flipped), flipped], axis=1).astype(BF16)
            qg = qg + dot(both, kr * head_mask(h, QUERY_WIDTH, KEY_SIZE))
            qs = slice(h * KEY_SIZE, (h + 1) * KEY_SIZE)
            t = LOGIT_SCALE * dot(qt[qs], both)
            tq_ref[qs] += t[:, : 2 * length]
            kg.append(t[:, 2 * length :])
            ds = slice(h * VALUE_SIZE, (h + 1) * VALUE_SIZE)
            u = dot(dt[ds], w_ref[n, h])
            tv_ref[ds] += u[:, : 2 * length]
            vg.append(u[:, 2 * length :])
        qg = dot(flip, (LOGIT_SCALE * qg).astype(BF16))
        kg = jnp.concatenate(kg, axis=0).T
        vg = jnp.concatenate(vg, axis=0).T
        gx = jnp.concatenate([qg, kg, vg], axis=1).astype(BF16)
        for i in range(gx_ref.shape[0]):
            gx_ref[i, n] = gx[i * tile : (i + 1) * tile]
        send(n)
        return carry

    lax.fori_loop(0, lines, line, 0)


def column_pass(qk_ref, u_ref, g_ref, rq_ref, rv_ref, gqk_ref, du_ref, tq_ref, tv_ref):
    columns, length, _ = qk_ref.shape
    rows = HEAD_COUNT * length
    flip_all = flip_matrix(rows, length)
    flip = flip_matrix(length, length)
    qmask = head_rows_mask(length, QUERY_WIDTH, KEY_SIZE)
    vmask = head_rows_mask(length, VALUE_WIDTH, VALUE_SIZE)
    tq_ref[...] = jnp.zeros_like(tq_ref)
    tv_ref[...] = jnp.zeros_like(tv_ref)

    def heads(x):
        return [x[h * length : (h + 1) * length] for h in range(HEAD_COUNT)]

    def absolute(s):
        shifted = [to_absolute(x) for x in heads(s[:, : 2 * length])]
        return s[:, 2 * length :] + jnp.concatenate(shifted, axis=0)

    def relative(flipped):
        shifted = [to_relative(x) for x in heads(flipped)]
        return jnp.concatenate([jnp.concatenate(shifted, axis=0), flipped], axis=1).astype(BF16)

    def column(c, carry):
        q, k = qk_ref[c, :, :QUERY_WIDTH], qk_ref[c, :, QUERY_WIDTH:]
        kr = jnp.concatenate([rq_ref[...], k], axis=0)
        us = jnp.concatenate([rv_ref[...], u_ref[pl.ds(c, length, stride=SUBLANES), :].astype(BF16)], axis=0)
        qs = jnp.concatenate([q] * HEAD_COUNT, axis=0) * qmask
        gs = jnp.concatenate([g_ref[c]] * HEAD_COUNT, axis=0) * vmask
        p = softmax(LOGIT_SCALE * absolute(dot_t(qs, kr)))
        g = absolute(dot_t(gs, us))
        e = p * (g - jnp.sum(p * g, axis=1, keepdims=True))
        e = relative(dot(flip_all, e.astype(BF16)))
        w = relative(dot(flip_all, p.astype(BF16)))
        parts = heads(dot(e, kr))
        qg = jnp.zeros((length, QUERY_WIDTH), F32)
        for h in range(HEAD_COUNT):
            qg = qg + parts[h] * head_mask(h, QUERY_WIDTH, KEY_SIZE).astype(F32)
        qg = dot(flip, (LOGIT_SCALE * qg).astype(BF16))
        qt = dot(flip_all, qs).T.astype(BF16)
        gt = dot(flip_all, gs).T.astype(BF16)
        t = LOGIT_SCALE * dot(qt, e)
        tq_ref[...] += t[:, : 2 * length]
        gqk_ref[c] = jnp.concatenate([qg, t[:, 2 * length :].T], axis=1).astype(BF16)
        t = dot(gt, w)
        tv_ref[...] += t[:, : 2 * length]
        du_ref[pl.ds(c, length, stride=SUBLANES), :] = t[:, 2 * length :].T.astype(BF16).astype(F32)
        return carry

    lax.fori_loop(0, columns, column, 0)


def peer_id(index, sizes):
    ha_size, wa_size = sizes
    return {"ha": index // wa_size, "wa": index % wa_size}


def greet(me, count, to_id):
    barrier = pltpu.get_barrier_semaphore()

    def signal(k, carry):
        pl.semaphore_signal(
            barrier,
            inc=1,
            device_id=to_id(lax.rem(me + k, count)),
            device_id_type=pl.DeviceIdType.MESH,
        )
        return carry

    lax.fori_loop(1, count, signal, 0)
    pl.semaphore_wait(barrier, count - 1)


def swap_all(me, count, to_id, source, target, send_sems, recv_sems, begin=True):
    def copy(peer, slot):
        return pltpu.make_async_remote_copy(
            src_ref=source(peer),
            dst_ref=target(slot),
            send_sem=send_sems.at[peer],
            recv_sem=recv_sems.at[slot],
            device_id=to_id(peer),
            device_id_type=pl.DeviceIdType.MESH,
        )

    def start(k, carry):
        copy(lax.rem(me + k, count), me).start()
        return carry

    def wait(k, carry):
        peer = lax.rem(me + k, count)
        copy(peer, peer).wait_recv()
        copy(peer, peer).wait_send()
        return carry

    def finish():
        lax.fori_loop(1, count, wait, 0)

    if begin:
        lax.fori_loop(1, count, start, 0)
    return finish


def pack_tables(tables, packed):
    wa_size, ha_size, per_device, rows, _ = packed.shape
    for w in range(wa_size):
        tiles = []
        for query, value in tables:
            for lane in range(0, query.shape[1], LANES):
                lanes = slice(lane, lane + LANES)
                tiles.append(query[w * rows : (w + 1) * rows, lanes])
                for start in range(w * VALUE_SIZE * rows // KEY_SIZE, (w + 1) * VALUE_SIZE * rows // KEY_SIZE, rows):
                    tiles.append(value[start : start + rows, lanes])
        for t in range(ha_size * per_device):
            tile = tiles[t] if t < len(tiles) else jnp.zeros((rows, LANES), F32)
            packed[w, t // per_device, t % per_device] = tile.astype(BF16)


def unpack_tables(summed, outs):
    per_device = summed.shape[1]
    parts = VALUE_SIZE // KEY_SIZE
    t = 0
    for query, value in outs:
        for lane in range(0, query.shape[0], LANES):
            count = min(LANES, query.shape[0] - lane)
            got = [summed[(t + i) // per_device, (t + i) % per_device] for i in range(1 + parts)]
            query[lane : lane + count, :] = got[0].T[:count]
            value[lane : lane + count, :] = jnp.concatenate(got[1:], axis=0).T[:count]
            t += 1 + parts


def layer_kernel(
    sizes,
    x_ref, rq_ref, rv_ref, qk_ref, g_ref, cq_ref, cv_ref,
    gx_ref, gqk_ref, tq_ref, tv_ref, ctq_ref, ctv_ref,
    x_lines, p_ref, w_ref, out_lines, values, grads, d_lines, gx_lines,
    row_query, row_value, column_query, column_value, packed, got, summed,
    x_send, x_recv, b_send, b_recv, c_send, c_recv, g_send, g_recv, t_send, t_recv, s_send, s_recv,
):
    ha_size, wa_size = sizes
    count = ha_size * wa_size
    ha, wa = lax.axis_index("ha"), lax.axis_index("wa")
    me = ha * wa_size + wa
    to_id = lambda i: peer_id(i, sizes)
    to_wa = lambda i: {"ha": ha, "wa": i}
    lines = x_lines.shape[1]
    height = values.shape[0]
    greet(me, count, to_id)

    finish = swap_all(
        wa,
        wa_size,
        to_wa,
        lambda i: x_ref.at[pl.ds(i * lines, lines)],
        lambda i: x_lines.at[i],
        x_send,
        x_recv,
    )
    x_lines[wa] = x_ref[pl.ds(wa * lines, lines)]
    finish()
    row_forward(x_lines, rq_ref, rv_ref, out_lines, p_ref, w_ref)

    finish = swap_all(
        me,
        count,
        to_id,
        lambda i: out_lines.at[i],
        lambda i: values.at[pl.ds(i * lines, lines)],
        b_send,
        b_recv,
    )
    values[pl.ds(me * lines, lines)] = out_lines[me]
    finish()
    column_pass(
        qk_ref,
        values.reshape(height * SUBLANES, VALUE_WIDTH),
        g_ref,
        cq_ref,
        cv_ref,
        gqk_ref,
        grads.reshape(height * SUBLANES, VALUE_WIDTH),
        column_query,
        column_value,
    )

    finish = swap_all(
        me,
        count,
        to_id,
        lambda i: grads.at[pl.ds(i * lines, lines)],
        lambda i: d_lines.at[i],
        c_send,
        c_recv,
    )
    d_lines[me] = grads[pl.ds(me * lines, lines)]
    finish()

    def swap_line(n, begin):
        return swap_all(
            wa,
            wa_size,
            to_wa,
            lambda i: gx_lines.at[i, n],
            lambda i: gx_ref.at[i * lines + n],
            g_send.at[n],
            g_recv.at[n],
            begin,
        )

    def send(n):
        swap_line(n, True)
        gx_ref[wa * lines + n] = gx_lines[wa, n]

    row_backward(
        x_lines, d_lines, p_ref, w_ref, rq_ref, rv_ref, gx_lines, row_query, row_value, send
    )
    pack_tables([(row_query, row_value), (column_query, column_value)], packed)
    finish = swap_all(
        me,
        count,
        to_id,
        lambda i: packed.at[i % wa_size, i // wa_size],
        lambda i: got.at[i],
        t_send,
        t_recv,
    )
    got[me] = packed[wa, ha]
    finish()
    summed[ha] = lax.fori_loop(
        0, count, lambda i, t: t + got[i].astype(F32), jnp.zeros(got.shape[1:], F32)
    )
    finish = swap_all(
        ha,
        ha_size,
        lambda i: {"ha": i, "wa": wa},
        lambda i: summed.at[ha],
        lambda i: summed.at[i],
        s_send,
        s_recv,
    )
    finish()
    unpack_tables(summed, [(tq_ref, tv_ref), (ctq_ref, ctv_ref)])

    def finish_lines(n, carry):
        swap_line(n, False)()
        return carry

    lax.fori_loop(0, lines, finish_lines, 0)


def layer(x, rq, rv, qk, g, cq, cv):
    sizes = (lax.axis_size("ha"), lax.axis_size("wa"))
    ha_size, wa_size = sizes
    count = ha_size * wa_size
    tile_rows, tile, channels = x.shape
    lines, length = tile_rows // wa_size, tile * wa_size
    columns, height, _ = qk.shape
    rows = QUERY_WIDTH // wa_size
    tiles = (1 + VALUE_SIZE // KEY_SIZE) * 2 * (length + height) // LANES
    per_device = -(-tiles // ha_size)
    operands = (x, rq, rv, qk, g, cq, cv)
    out_shapes = [
        (x.shape, BF16),
        (qk.shape, BF16),
        ((2 * length - 1, rows), F32),
        ((2 * length - 1, VALUE_WIDTH // wa_size), F32),
        ((2 * height - 1, rows), F32),
        ((2 * height - 1, VALUE_WIDTH // wa_size), F32),
    ]
    scratch = [
        ((wa_size, lines, tile, channels), BF16),
        ((lines, HEAD_COUNT, length, length), F32),
        ((lines, HEAD_COUNT, length, 3 * length), BF16),
        ((count, lines, SUBLANES, VALUE_WIDTH), F32),
        ((height, SUBLANES, VALUE_WIDTH), F32),
        ((height, SUBLANES, VALUE_WIDTH), F32),
        ((count, lines, SUBLANES, VALUE_WIDTH), F32),
        ((wa_size, lines, tile, channels), BF16),
        ((QUERY_WIDTH, 2 * length), F32),
        ((VALUE_WIDTH, 2 * length), F32),
        ((QUERY_WIDTH, 2 * height), F32),
        ((VALUE_WIDTH, 2 * height), F32),
        ((wa_size, ha_size, per_device, rows, LANES), BF16),
        ((count, per_device, rows, LANES), BF16),
        ((ha_size, per_device, rows, LANES), F32),
    ]
    semaphores = [(wa_size,), (count,), (count,), (lines, wa_size), (count,), (ha_size,)]
    return pl.pallas_call(
        functools.partial(layer_kernel, sizes),
        name="layer",
        out_shape=[jax.ShapeDtypeStruct(s, t) for s, t in out_shapes],
        in_specs=[pl.BlockSpec(memory_space=pltpu.VMEM)] * len(operands),
        out_specs=[pl.BlockSpec(memory_space=pltpu.VMEM)] * len(out_shapes),
        scratch_shapes=[pltpu.VMEM(s, t) for s, t in scratch]
        + [pltpu.SemaphoreType.DMA(s) for s in semaphores for _ in range(2)],
        compiler_params=pltpu.CompilerParams(
            collective_id=0, has_side_effects=True, vmem_limit_bytes=56 * 1024 * 1024
        ),
    )(*operands)


def on_device(
    row_features,
    row_table_query,
    row_table_value,
    column_query_key,
    column_table_query,
    column_table_value,
    output_cotangent,
):
    pad = lambda t: jnp.pad(t, ((0, 1), (0, 0)))
    outs = layer(
        row_features,
        pad(row_table_query),
        pad(row_table_value),
        column_query_key.swapaxes(0, 1),
        output_cotangent.swapaxes(0, 1),
        pad(column_table_query),
        pad(column_table_value),
    )
    return (outs[0], outs[1].swapaxes(0, 1), *outs[2:])


def solution(mesh):
    placed = (
        P("ha", "wa", None),
        P(),
        P(),
        P(None, ("ha", "wa"), None),
        P(),
        P(),
        P(None, ("ha", "wa"), None),
    )
    return jax.shard_map(
        on_device,
        mesh=mesh,
        in_specs=placed,
        out_specs=(
            P("ha", "wa", None),
            P(None, ("ha", "wa"), None),
            P(None, "wa"),
            P(None, "wa"),
            P(None, "wa"),
            P(None, "wa"),
        ),
        check_vma=False,
    )
```

```python
import functools

import jax
import jax.numpy as jnp
from jax import lax
from jax.experimental import pallas as pl
from jax.experimental.pallas import tpu as pltpu
from jax.sharding import PartitionSpec as P

HEAD_COUNT = 4
KEY_SIZE = 16
VALUE_SIZE = 32
QUERY_WIDTH = HEAD_COUNT * KEY_SIZE
VALUE_WIDTH = HEAD_COUNT * VALUE_SIZE
LOGIT_SCALE = KEY_SIZE ** (-0.5)
F32 = jnp.float32
BF16 = jnp.bfloat16
SUBLANES = 8
LANES = 128


def dot(a, b):
    return lax.dot_general(a, b, (((1,), (0,)), ((), ())), preferred_element_type=F32)


def dot_t(a, b):
    return lax.dot_general(a, b, (((1,), (1,)), ((), ())), preferred_element_type=F32)


def flip_matrix(length, block):
    i = lax.broadcasted_iota(jnp.int32, (length, length), 0)
    j = lax.broadcasted_iota(jnp.int32, (length, length), 1)
    same = (i // block == j // block) & (i % block + j % block == block - 1)
    return jnp.where(same, 1.0, 0.0).astype(BF16)


def head_mask(head, width, per_head):
    lane = lax.broadcasted_iota(jnp.int32, (1, width), 1)
    return jnp.where(lane // per_head == head, 1.0, 0.0).astype(BF16)


def head_rows_mask(length, width, per_head):
    shape = (HEAD_COUNT * length, width)
    row = lax.broadcasted_iota(jnp.int32, shape, 0)
    lane = lax.broadcasted_iota(jnp.int32, shape, 1)
    return jnp.where(lane // per_head == row // length, 1.0, 0.0).astype(BF16)


def to_absolute(table):
    length = table.shape[0]
    return pltpu.roll(table, length + 1, 1, stride=1, stride_axis=0)[:, :length]


def to_relative(flipped):
    padded = jnp.concatenate([flipped, jnp.zeros_like(flipped)], axis=1)
    return pltpu.roll(padded, 0, 1, stride=1, stride_axis=0)


def softmax(logits):
    e = jnp.exp(logits - jnp.max(logits, axis=1, keepdims=True))
    return e * (1.0 / jnp.sum(e, axis=1, keepdims=True))


def row_forward(x_ref, rq_ref, rv_ref, out_ref, p_ref, w_ref, receive, send):
    lines = x_ref.shape[1]
    length = p_ref.shape[2]
    columns = length // out_ref.shape[0]
    flip = flip_matrix(length, length)

    def line(n, carry):
        receive(n)
        x = jnp.concatenate([x_ref[i, n] for i in range(x_ref.shape[0])], axis=0)
        q, k, v = x[:, :QUERY_WIDTH], x[:, QUERY_WIDTH : 2 * QUERY_WIDTH], x[:, 2 * QUERY_WIDTH :]
        kr = jnp.concatenate([rq_ref[...], k], axis=0)
        vs = jnp.concatenate([rv_ref[...], v], axis=0)
        out = jnp.zeros((length, VALUE_WIDTH), F32)
        for h in range(HEAD_COUNT):
            s = dot_t(q * head_mask(h, QUERY_WIDTH, KEY_SIZE), kr)
            p = softmax(
                LOGIT_SCALE * (s[:, 2 * length :] + to_absolute(s[:, : 2 * length]))
            )
            p_ref[n, h] = p
            flipped = dot(flip, p.astype(BF16))
            both = jnp.concatenate([to_relative(flipped), flipped], axis=1).astype(BF16)
            w_ref[n, h] = both
            out = out + dot(both, vs * head_mask(h, VALUE_WIDTH, VALUE_SIZE))
        out = dot(flip, out.astype(BF16))
        for i in range(out_ref.shape[0]):
            out_ref[i, n, :columns] = out[i * columns : (i + 1) * columns].astype(BF16)
        send(n)
        return carry

    lax.fori_loop(0, lines, line, 0)


def row_backward(x_ref, d_ref, p_ref, w_ref, rq_ref, rv_ref, gx_ref, tq_ref, tv_ref, send):
    lines = x_ref.shape[1]
    length = p_ref.shape[2]
    columns = length // d_ref.shape[0]
    tile = gx_ref.shape[2]
    flip = flip_matrix(length, length)
    tq_ref[...] = jnp.zeros_like(tq_ref)
    tv_ref[...] = jnp.zeros_like(tv_ref)

    def line(n, carry):
        x = jnp.concatenate([x_ref[i, n] for i in range(x_ref.shape[0])], axis=0)
        d = [d_ref[i, n].astype(F32)[:columns] for i in range(d_ref.shape[0])]
        d = jnp.concatenate(d, axis=0).astype(BF16)
        q, k, v = x[:, :QUERY_WIDTH], x[:, QUERY_WIDTH : 2 * QUERY_WIDTH], x[:, 2 * QUERY_WIDTH :]
        kr = jnp.concatenate([rq_ref[...], k], axis=0)
        vs = jnp.concatenate([rv_ref[...], v], axis=0)
        qt = dot(flip, q).T.astype(BF16)
        dt = dot(flip, d).T.astype(BF16)
        qg = jnp.zeros((length, QUERY_WIDTH), F32)
        kg, vg = [], []
        for h in range(HEAD_COUNT):
            g = dot_t(d * head_mask(h, VALUE_WIDTH, VALUE_SIZE), vs)
            g = g[:, 2 * length :] + to_absolute(g[:, : 2 * length])
            p = p_ref[n, h]
            e = p * (g - jnp.sum(p * g, axis=1, keepdims=True))
            flipped = dot(flip, e.astype(BF16))
            both = jnp.concatenate([to_relative(flipped), flipped], axis=1).astype(BF16)
            qg = qg + dot(both, kr * head_mask(h, QUERY_WIDTH, KEY_SIZE))
            qs = slice(h * KEY_SIZE, (h + 1) * KEY_SIZE)
            t = LOGIT_SCALE * dot(qt[qs], both)
            tq_ref[qs] += t[:, : 2 * length]
            kg.append(t[:, 2 * length :])
            ds = slice(h * VALUE_SIZE, (h + 1) * VALUE_SIZE)
            u = dot(dt[ds], w_ref[n, h])
            tv_ref[ds] += u[:, : 2 * length]
            vg.append(u[:, 2 * length :])
        qg = dot(flip, (LOGIT_SCALE * qg).astype(BF16))
        kg = jnp.concatenate(kg, axis=0).T
        vg = jnp.concatenate(vg, axis=0).T
        gx = jnp.concatenate([qg, kg, vg], axis=1).astype(BF16)
        for i in range(gx_ref.shape[0]):
            gx_ref[i, n] = gx[i * tile : (i + 1) * tile]
        send(n)
        return carry

    lax.fori_loop(0, lines, line, 0)


def column_pass(columns, qk_ref, u_ref, g_ref, rq_ref, rv_ref, gqk_ref, du_ref, tq_ref, tv_ref):
    length = qk_ref.shape[0] // SUBLANES
    rows = HEAD_COUNT * length
    flip_all = flip_matrix(rows, length)
    flip = flip_matrix(length, length)
    qmask = head_rows_mask(length, QUERY_WIDTH, KEY_SIZE)
    vmask = head_rows_mask(length, VALUE_WIDTH, VALUE_SIZE)
    tq_ref[...] = jnp.zeros_like(tq_ref)
    tv_ref[...] = jnp.zeros_like(tv_ref)

    def heads(x):
        return [x[h * length : (h + 1) * length] for h in range(HEAD_COUNT)]

    def absolute(s):
        shifted = [to_absolute(x) for x in heads(s[:, : 2 * length])]
        return s[:, 2 * length :] + jnp.concatenate(shifted, axis=0)

    def relative(flipped):
        shifted = [to_relative(x) for x in heads(flipped)]
        return jnp.concatenate([jnp.concatenate(shifted, axis=0), flipped], axis=1).astype(BF16)

    def column(c, carry):
        cells = pl.ds(c, length, stride=SUBLANES)
        qk = qk_ref[cells, :].astype(BF16)
        q, k = qk[:, :QUERY_WIDTH], qk[:, QUERY_WIDTH:]
        kr = jnp.concatenate([rq_ref[...], k], axis=0)
        us = jnp.concatenate([rv_ref[...], u_ref[cells, :].astype(BF16)], axis=0)
        qs = jnp.concatenate([q] * HEAD_COUNT, axis=0) * qmask
        gs = jnp.concatenate([g_ref[cells, :].astype(BF16)] * HEAD_COUNT, axis=0) * vmask
        p = softmax(LOGIT_SCALE * absolute(dot_t(qs, kr)))
        g = absolute(dot_t(gs, us))
        e = p * (g - jnp.sum(p * g, axis=1, keepdims=True))
        e = relative(dot(flip_all, e.astype(BF16)))
        w = relative(dot(flip_all, p.astype(BF16)))
        parts = heads(dot(e, kr))
        qg = jnp.zeros((length, QUERY_WIDTH), F32)
        for h in range(HEAD_COUNT):
            qg = qg + parts[h] * head_mask(h, QUERY_WIDTH, KEY_SIZE).astype(F32)
        qg = dot(flip, (LOGIT_SCALE * qg).astype(BF16))
        qt = dot(flip_all, qs).T.astype(BF16)
        gt = dot(flip_all, gs).T.astype(BF16)
        t = LOGIT_SCALE * dot(qt, e)
        tq_ref[...] += t[:, : 2 * length]
        gqk_ref[cells, :] = jnp.concatenate([qg, t[:, 2 * length :].T], axis=1)
        t = dot(gt, w)
        tv_ref[...] += t[:, : 2 * length]
        du_ref[cells, :] = t[:, 2 * length :].T
        return carry

    lax.fori_loop(0, columns, column, 0)


def peer_id(index, sizes):
    ha_size, wa_size = sizes
    return {"ha": index // wa_size, "wa": index % wa_size}


def greet(me, count, to_id):
    barrier = pltpu.get_barrier_semaphore()

    def signal(k, carry):
        pl.semaphore_signal(
            barrier,
            inc=1,
            device_id=to_id(lax.rem(me + k, count)),
            device_id_type=pl.DeviceIdType.MESH,
        )
        return carry

    lax.fori_loop(1, count, signal, 0)
    pl.semaphore_wait(barrier, count - 1)


def swap_all(me, count, to_id, source, target, send_sems, recv_sems, begin=True):
    def copy(peer, slot):
        return pltpu.make_async_remote_copy(
            src_ref=source(peer),
            dst_ref=target(slot),
            send_sem=send_sems.at[peer],
            recv_sem=recv_sems.at[slot],
            device_id=to_id(peer),
            device_id_type=pl.DeviceIdType.MESH,
        )

    def start(k, carry):
        copy(lax.rem(me + k, count), me).start()
        return carry

    def wait(k, carry):
        peer = lax.rem(me + k, count)
        copy(peer, peer).wait_recv()
        copy(peer, peer).wait_send()
        return carry

    def finish():
        lax.fori_loop(1, count, wait, 0)

    if begin:
        lax.fori_loop(1, count, start, 0)
    return finish


def pack_tables(tables, packed):
    ha_size, wa_size, per_device, rows, _ = packed.shape
    for w in range(wa_size):
        tiles = []
        for query, value in tables:
            for lane in range(0, query.shape[1], LANES):
                lanes = slice(lane, lane + LANES)
                tiles.append(query[w * rows : (w + 1) * rows, lanes])
                for start in range(w * VALUE_SIZE * rows // KEY_SIZE, (w + 1) * VALUE_SIZE * rows // KEY_SIZE, rows):
                    tiles.append(value[start : start + rows, lanes])
        for t in range(ha_size * per_device):
            tile = tiles[t] if t < len(tiles) else jnp.zeros((rows, LANES), F32)
            packed[t // per_device, w, t % per_device] = tile.astype(BF16)


def unpack_tables(summed, outs):
    per_device = summed.shape[1]
    parts = VALUE_SIZE // KEY_SIZE
    t = 0
    for query, value in outs:
        for lane in range(0, query.shape[1], LANES):
            count = min(LANES, query.shape[1] - lane)
            got = [summed[(t + i) // per_device, (t + i) % per_device] for i in range(1 + parts)]
            query[:, lane : lane + count] = got[0][:, :count]
            value[:, lane : lane + count] = jnp.concatenate(got[1:], axis=0)[:, :count]
            t += 1 + parts


def fill_table(table_ref, padded, turn):
    padded[...] = jnp.zeros_like(padded)
    padded[: padded.shape[0] - 1, :] = (
        table_ref[...].astype(F32).T.astype(BF16) if turn else table_ref[...]
    )


def layer_kernel(
    sizes,
    x_ref, rq_in, rv_in, qk_ref, g_ref, cq_in, cv_in,
    gx_ref, gqk_ref, tq_ref, tv_ref, ctq_ref, ctv_ref,
    rq_ref, rv_ref, cq_ref, cv_ref, qk_cells, g_cells, gqk_cells,
    x_lines, p_ref, w_ref, out_lines, values_in, values, grads, grads_out, d_lines, gx_lines,
    row_query, row_value, column_query, column_value, packed, got, part, got_part, summed,
    x_send, x_recv, b_send, b_recv, c_send, c_recv, g_send, g_recv, t_send, t_recv,
    u_send, u_recv, s_send, s_recv,
):
    ha_size, wa_size = sizes
    count = ha_size * wa_size
    ha, wa = lax.axis_index("ha"), lax.axis_index("wa")
    me = ha * wa_size + wa
    to_id = lambda i: peer_id(i, sizes)
    to_wa = lambda i: {"ha": ha, "wa": i}
    lines = x_lines.shape[1]
    height = values.shape[0]
    columns = qk_ref.shape[1]
    greet(me, count, to_id)

    def swap_x(n, begin):
        return swap_all(
            wa,
            wa_size,
            to_wa,
            lambda i: x_ref.at[i * lines + n],
            lambda i: x_lines.at[i, n],
            x_send.at[n],
            x_recv.at[n],
            begin,
        )

    def swap_b(n, begin):
        return swap_all(
            me,
            count,
            to_id,
            lambda i: out_lines.at[i, n],
            lambda i: values_in.at[i * lines + n],
            b_send.at[n],
            b_recv.at[n],
            begin,
        )

    def each_line(step):
        def body(n, carry):
            step(n)
            return carry

        lax.fori_loop(0, lines, body, 0)

    each_line(lambda n: swap_x(n, True))
    x_lines[wa] = x_ref[pl.ds(wa * lines, lines)]
    fill_table(rq_in, rq_ref, True)
    fill_table(rv_in, rv_ref, False)
    fill_table(cq_in, cq_ref, True)
    fill_table(cv_in, cv_ref, False)
    qk_cells[:, :columns] = qk_ref[...].astype(F32)
    g_cells[:, :columns] = g_ref[...].astype(F32)

    def send_b(n):
        swap_b(n, True)
        values_in[me * lines + n] = out_lines[me, n]

    row_forward(
        x_lines, rq_ref, rv_ref, out_lines, p_ref, w_ref, lambda n: swap_x(n, False)(), send_b
    )
    each_line(lambda n: swap_b(n, False)())
    values[...] = values_in[...].astype(F32)
    cells = lambda ref: ref.reshape(height * SUBLANES, VALUE_WIDTH)
    column_pass(
        columns,
        cells(qk_cells),
        cells(values),
        cells(g_cells),
        cq_ref,
        cv_ref,
        cells(gqk_cells),
        cells(grads),
        column_query,
        column_value,
    )
    grads_out[...] = grads[...].astype(BF16)

    finish = swap_all(
        me,
        count,
        to_id,
        lambda i: grads_out.at[pl.ds(i * lines, lines)],
        lambda i: d_lines.at[i],
        c_send,
        c_recv,
    )
    d_lines[me] = grads_out[pl.ds(me * lines, lines)]
    gqk_ref[...] = gqk_cells[:, :columns].astype(BF16)
    finish()

    def swap_line(n, begin):
        return swap_all(
            wa,
            wa_size,
            to_wa,
            lambda i: gx_lines.at[i, n],
            lambda i: gx_ref.at[i * lines + n],
            g_send.at[n],
            g_recv.at[n],
            begin,
        )

    def send(n):
        swap_line(n, True)
        gx_ref[wa * lines + n] = gx_lines[wa, n]

    row_backward(
        x_lines, d_lines, p_ref, w_ref, rq_ref, rv_ref, gx_lines, row_query, row_value, send
    )
    pack_tables([(row_query, row_value), (column_query, column_value)], packed)
    to_ha = lambda i: {"ha": i, "wa": wa}
    finish = swap_all(
        ha, ha_size, to_ha, lambda i: packed.at[i], lambda i: got.at[i], t_send, t_recv
    )
    got[ha] = packed[ha]
    finish()
    total = got[0].astype(F32)
    for i in range(1, ha_size):
        total = total + got[i].astype(F32)
    part[...] = total
    finish = swap_all(
        wa, wa_size, to_wa, lambda i: part.at[i], lambda i: got_part.at[i], u_send, u_recv
    )
    got_part[wa] = part[wa]
    finish()
    total = got_part[0]
    for i in range(1, wa_size):
        total = total + got_part[i]
    summed[ha] = total
    finish = swap_all(
        ha,
        ha_size,
        to_ha,
        lambda i: summed.at[ha],
        lambda i: summed.at[i],
        s_send,
        s_recv,
    )
    finish()
    unpack_tables(summed, [(tq_ref, tv_ref), (ctq_ref, ctv_ref)])

    each_line(lambda n: swap_line(n, False)())


def layer(x, rq, rv, qk, g, cq, cv):
    sizes = (lax.axis_size("ha"), lax.axis_size("wa"))
    ha_size, wa_size = sizes
    count = ha_size * wa_size
    tile_rows, tile, channels = x.shape
    lines, length = tile_rows // wa_size, tile * wa_size
    height, columns, _ = qk.shape
    rows = QUERY_WIDTH // wa_size
    tiles = (1 + VALUE_SIZE // KEY_SIZE) * 2 * (length + height) // LANES
    per_device = -(-tiles // ha_size)
    operands = (x, rq, rv, qk, g, cq, cv)
    out_shapes = [
        (x.shape, BF16),
        (qk.shape, BF16),
        ((rows, 2 * length - 1), F32),
        ((VALUE_WIDTH // wa_size, 2 * length - 1), F32),
        ((rows, 2 * height - 1), F32),
        ((VALUE_WIDTH // wa_size, 2 * height - 1), F32),
    ]
    scratch = [
        ((2 * length, QUERY_WIDTH), BF16),
        ((2 * length, VALUE_WIDTH), BF16),
        ((2 * height, QUERY_WIDTH), BF16),
        ((2 * height, VALUE_WIDTH), BF16),
        ((height, SUBLANES, VALUE_WIDTH), F32),
        ((height, SUBLANES, VALUE_WIDTH), F32),
        ((height, SUBLANES, VALUE_WIDTH), F32),
        ((wa_size, lines, tile, channels), BF16),
        ((lines, HEAD_COUNT, length, length), F32),
        ((lines, HEAD_COUNT, length, 3 * length), BF16),
        ((count, lines, SUBLANES, VALUE_WIDTH), BF16),
        ((height, SUBLANES, VALUE_WIDTH), BF16),
        ((height, SUBLANES, VALUE_WIDTH), F32),
        ((height, SUBLANES, VALUE_WIDTH), F32),
        ((height, SUBLANES, VALUE_WIDTH), BF16),
        ((count, lines, SUBLANES, VALUE_WIDTH), BF16),
        ((wa_size, lines, tile, channels), BF16),
        ((QUERY_WIDTH, 2 * length), F32),
        ((VALUE_WIDTH, 2 * length), F32),
        ((QUERY_WIDTH, 2 * height), F32),
        ((VALUE_WIDTH, 2 * height), F32),
        ((ha_size, wa_size, per_device, rows, LANES), BF16),
        ((ha_size, wa_size, per_device, rows, LANES), BF16),
        ((wa_size, per_device, rows, LANES), F32),
        ((wa_size, per_device, rows, LANES), F32),
        ((ha_size, per_device, rows, LANES), F32),
    ]
    semaphores = [
        (lines, wa_size),
        (lines, count),
        (count,),
        (lines, wa_size),
        (ha_size,),
        (wa_size,),
        (ha_size,),
    ]
    return pl.pallas_call(
        functools.partial(layer_kernel, sizes),
        name="layer",
        out_shape=[jax.ShapeDtypeStruct(s, t) for s, t in out_shapes],
        in_specs=[pl.BlockSpec(memory_space=pltpu.VMEM)] * len(operands),
        out_specs=[pl.BlockSpec(memory_space=pltpu.VMEM)] * len(out_shapes),
        scratch_shapes=[pltpu.VMEM(s, t) for s, t in scratch]
        + [pltpu.SemaphoreType.DMA(s) for s in semaphores for _ in range(2)],
        compiler_params=pltpu.CompilerParams(
            collective_id=0, has_side_effects=True, vmem_limit_bytes=56 * 1024 * 1024
        ),
    )(*operands)


def on_device(
    row_features,
    row_table_query,
    row_table_value,
    column_query_key,
    column_table_query,
    column_table_value,
    output_cotangent,
):
    outs = layer(
        row_features,
        row_table_query.T,
        row_table_value,
        column_query_key,
        output_cotangent,
        column_table_query.T,
        column_table_value,
    )
    return (outs[0], outs[1], *(t.T for t in outs[2:]))


def solution(mesh):
    placed = (
        P("ha", "wa", None),
        P(),
        P(),
        P(None, ("ha", "wa"), None),
        P(),
        P(),
        P(None, ("ha", "wa"), None),
    )
    return jax.shard_map(
        on_device,
        mesh=mesh,
        in_specs=placed,
        out_specs=(
            P("ha", "wa", None),
            P(None, ("ha", "wa"), None),
            P(None, "wa"),
            P(None, "wa"),
            P(None, "wa"),
            P(None, "wa"),
        ),
        check_vma=False,
    )
```

```python
import functools

import jax
import jax.numpy as jnp
from jax import lax
from jax.experimental import pallas as pl
from jax.experimental.pallas import tpu as pltpu
from jax.sharding import PartitionSpec as P

HEAD_COUNT = 4
KEY_SIZE = 16
VALUE_SIZE = 32
QUERY_WIDTH = HEAD_COUNT * KEY_SIZE
VALUE_WIDTH = HEAD_COUNT * VALUE_SIZE
LOGIT_SCALE = KEY_SIZE ** (-0.5)
F32 = jnp.float32
BF16 = jnp.bfloat16
SUBLANES = 8
LANES = 128


def dot(a, b):
    return lax.dot_general(a, b, (((1,), (0,)), ((), ())), preferred_element_type=F32)


def dot_t(a, b):
    return lax.dot_general(a, b, (((1,), (1,)), ((), ())), preferred_element_type=F32)


def flip_matrix(length, block):
    i = lax.broadcasted_iota(jnp.int32, (length, length), 0)
    j = lax.broadcasted_iota(jnp.int32, (length, length), 1)
    same = (i // block == j // block) & (i % block + j % block == block - 1)
    return jnp.where(same, 1.0, 0.0).astype(BF16)


def head_mask(head, width, per_head):
    lane = lax.broadcasted_iota(jnp.int32, (1, width), 1)
    return jnp.where(lane // per_head == head, 1.0, 0.0).astype(BF16)


def head_rows_mask(length, width, per_head):
    shape = (HEAD_COUNT * length, width)
    row = lax.broadcasted_iota(jnp.int32, shape, 0)
    lane = lax.broadcasted_iota(jnp.int32, shape, 1)
    return jnp.where(lane // per_head == row // length, 1.0, 0.0).astype(BF16)


def to_absolute(table):
    length = table.shape[0]
    return pltpu.roll(table, length + 1, 1, stride=1, stride_axis=0)[:, :length]


def to_relative(flipped):
    padded = jnp.concatenate([flipped, jnp.zeros_like(flipped)], axis=1)
    return pltpu.roll(padded, 0, 1, stride=1, stride_axis=0)


def softmax(logits):
    e = jnp.exp(logits - jnp.max(logits, axis=1, keepdims=True))
    return e * (1.0 / jnp.sum(e, axis=1, keepdims=True))


def row_forward(x_ref, rq_ref, rv_ref, out_ref, p_ref, w_ref, receive, send):
    lines = x_ref.shape[1]
    length = p_ref.shape[2]
    columns = length // out_ref.shape[0]
    flip = flip_matrix(length, length)

    def line(n, carry):
        receive(n)
        x = jnp.concatenate([x_ref[i, n] for i in range(x_ref.shape[0])], axis=0)
        q, k, v = x[:, :QUERY_WIDTH], x[:, QUERY_WIDTH : 2 * QUERY_WIDTH], x[:, 2 * QUERY_WIDTH :]
        kr = jnp.concatenate([rq_ref[...], k], axis=0)
        vs = jnp.concatenate([rv_ref[...], v], axis=0)
        out = jnp.zeros((length, VALUE_WIDTH), F32)
        for h in range(HEAD_COUNT):
            s = dot_t(q * head_mask(h, QUERY_WIDTH, KEY_SIZE), kr)
            p = softmax(
                LOGIT_SCALE * (s[:, 2 * length :] + to_absolute(s[:, : 2 * length]))
            )
            p_ref[n, h] = p
            flipped = dot(flip, p.astype(BF16))
            both = jnp.concatenate([to_relative(flipped), flipped], axis=1).astype(BF16)
            w_ref[n, h] = both
            out = out + dot(both, vs * head_mask(h, VALUE_WIDTH, VALUE_SIZE))
        out = dot(flip, out.astype(BF16))
        for i in range(out_ref.shape[0]):
            out_ref[i, n, :columns] = out[i * columns : (i + 1) * columns].astype(BF16)
        send(n)
        return carry

    lax.fori_loop(0, lines, line, 0)


def row_backward(x_ref, d_ref, p_ref, w_ref, rq_ref, rv_ref, gx_ref, tq_ref, tv_ref, send):
    lines = x_ref.shape[1]
    length = p_ref.shape[2]
    columns = length // d_ref.shape[0]
    tile = gx_ref.shape[2]
    flip = flip_matrix(length, length)
    tq_ref[...] = jnp.zeros_like(tq_ref)
    tv_ref[...] = jnp.zeros_like(tv_ref)

    def line(n, carry):
        x = jnp.concatenate([x_ref[i, n] for i in range(x_ref.shape[0])], axis=0)
        d = [d_ref[i, n].astype(F32)[:columns] for i in range(d_ref.shape[0])]
        d = jnp.concatenate(d, axis=0).astype(BF16)
        q, k, v = x[:, :QUERY_WIDTH], x[:, QUERY_WIDTH : 2 * QUERY_WIDTH], x[:, 2 * QUERY_WIDTH :]
        kr = jnp.concatenate([rq_ref[...], k], axis=0)
        vs = jnp.concatenate([rv_ref[...], v], axis=0)
        qt = dot(flip, q).T.astype(BF16)
        dt = dot(flip, d).T.astype(BF16)
        qg = jnp.zeros((length, QUERY_WIDTH), F32)
        kg, vg = [], []
        for h in range(HEAD_COUNT):
            g = dot_t(d * head_mask(h, VALUE_WIDTH, VALUE_SIZE), vs)
            g = g[:, 2 * length :] + to_absolute(g[:, : 2 * length])
            p = p_ref[n, h]
            e = p * (g - jnp.sum(p * g, axis=1, keepdims=True))
            flipped = dot(flip, e.astype(BF16))
            both = jnp.concatenate([to_relative(flipped), flipped], axis=1).astype(BF16)
            qg = qg + dot(both, kr * head_mask(h, QUERY_WIDTH, KEY_SIZE))
            qs = slice(h * KEY_SIZE, (h + 1) * KEY_SIZE)
            t = LOGIT_SCALE * dot(qt[qs], both)
            tq_ref[qs] += t[:, : 2 * length]
            kg.append(t[:, 2 * length :])
            ds = slice(h * VALUE_SIZE, (h + 1) * VALUE_SIZE)
            u = dot(dt[ds], w_ref[n, h])
            tv_ref[ds] += u[:, : 2 * length]
            vg.append(u[:, 2 * length :])
        qg = dot(flip, (LOGIT_SCALE * qg).astype(BF16))
        kg = jnp.concatenate(kg, axis=0).T
        vg = jnp.concatenate(vg, axis=0).T
        gx = jnp.concatenate([qg, kg, vg], axis=1).astype(BF16)
        for i in range(gx_ref.shape[0]):
            gx_ref[i, n] = gx[i * tile : (i + 1) * tile]
        send(n)
        return carry

    lax.fori_loop(0, lines, line, 0)


def column_pass(
    first, columns, qk_ref, u_ref, g_ref, rq_ref, rv_ref, gqk_ref, du_ref, tq_ref, tv_ref, p_ref
):
    length = qk_ref.shape[0] // SUBLANES
    rows = HEAD_COUNT * length
    flip_all = flip_matrix(rows, length)
    flip = flip_matrix(length, length)
    qmask = head_rows_mask(length, QUERY_WIDTH, KEY_SIZE)
    vmask = head_rows_mask(length, VALUE_WIDTH, VALUE_SIZE)
    if first:
        tv_ref[...] = jnp.zeros_like(tv_ref)
    else:
        tq_ref[...] = jnp.zeros_like(tq_ref)

    def heads(x):
        return [x[h * length : (h + 1) * length] for h in range(HEAD_COUNT)]

    def absolute(s):
        shifted = [to_absolute(x) for x in heads(s[:, : 2 * length])]
        return s[:, 2 * length :] + jnp.concatenate(shifted, axis=0)

    def relative(flipped):
        shifted = [to_relative(x) for x in heads(flipped)]
        return jnp.concatenate([jnp.concatenate(shifted, axis=0), flipped], axis=1).astype(BF16)

    def column(c, carry):
        cells = pl.ds(c, length, stride=SUBLANES)
        qk = qk_ref[cells, :].astype(BF16)
        q, k = qk[:, :QUERY_WIDTH], qk[:, QUERY_WIDTH:]
        kr = jnp.concatenate([rq_ref[...], k], axis=0)
        qs = jnp.concatenate([q] * HEAD_COUNT, axis=0) * qmask
        gs = jnp.concatenate([g_ref[cells, :].astype(BF16)] * HEAD_COUNT, axis=0) * vmask
        if first:
            p = softmax(LOGIT_SCALE * absolute(dot_t(qs, kr)))
            p_ref[c] = p
            w = relative(dot(flip_all, p.astype(BF16)))
            gt = dot(flip_all, gs).T.astype(BF16)
            t = dot(gt, w)
            tv_ref[...] += t[:, : 2 * length]
            du_ref[cells, :] = t[:, 2 * length :].T
            return carry
        us = jnp.concatenate([rv_ref[...], u_ref[cells, :].astype(BF16)], axis=0)
        p = p_ref[c]
        g = absolute(dot_t(gs, us))
        e = p * (g - jnp.sum(p * g, axis=1, keepdims=True))
        e = relative(dot(flip_all, e.astype(BF16)))
        parts = heads(dot(e, kr))
        qg = jnp.zeros((length, QUERY_WIDTH), F32)
        for h in range(HEAD_COUNT):
            qg = qg + parts[h] * head_mask(h, QUERY_WIDTH, KEY_SIZE).astype(F32)
        qg = dot(flip, (LOGIT_SCALE * qg).astype(BF16))
        qt = dot(flip_all, qs).T.astype(BF16)
        t = LOGIT_SCALE * dot(qt, e)
        tq_ref[...] += t[:, : 2 * length]
        gqk_ref[cells, :] = jnp.concatenate([qg, t[:, 2 * length :].T], axis=1)
        return carry

    lax.fori_loop(0, columns, column, 0)


def peer_id(index, sizes):
    ha_size, wa_size = sizes
    return {"ha": index // wa_size, "wa": index % wa_size}


def greet(me, count, to_id):
    barrier = pltpu.get_barrier_semaphore()

    def signal(k, carry):
        pl.semaphore_signal(
            barrier,
            inc=1,
            device_id=to_id(lax.rem(me + k, count)),
            device_id_type=pl.DeviceIdType.MESH,
        )
        return carry

    lax.fori_loop(1, count, signal, 0)
    pl.semaphore_wait(barrier, count - 1)


def swap_all(me, count, to_id, source, target, send_sems, recv_sems, begin=True):
    def copy(peer, slot):
        return pltpu.make_async_remote_copy(
            src_ref=source(peer),
            dst_ref=target(slot),
            send_sem=send_sems.at[peer],
            recv_sem=recv_sems.at[slot],
            device_id=to_id(peer),
            device_id_type=pl.DeviceIdType.MESH,
        )

    def start(k, carry):
        copy(lax.rem(me + k, count), me).start()
        return carry

    def wait(k, carry):
        peer = lax.rem(me + k, count)
        copy(peer, peer).wait_recv()
        copy(peer, peer).wait_send()
        return carry

    def finish():
        lax.fori_loop(1, count, wait, 0)

    if begin:
        lax.fori_loop(1, count, start, 0)
    return finish


def pack_tables(tables, packed):
    ha_size, wa_size, per_device, rows, _ = packed.shape
    for w in range(wa_size):
        tiles = []
        for query, value in tables:
            for lane in range(0, query.shape[1], LANES):
                lanes = slice(lane, lane + LANES)
                tiles.append(query[w * rows : (w + 1) * rows, lanes])
                for start in range(w * VALUE_SIZE * rows // KEY_SIZE, (w + 1) * VALUE_SIZE * rows // KEY_SIZE, rows):
                    tiles.append(value[start : start + rows, lanes])
        for t in range(ha_size * per_device):
            tile = tiles[t] if t < len(tiles) else jnp.zeros((rows, LANES), F32)
            packed[t // per_device, w, t % per_device] = tile.astype(BF16)


def unpack_tables(summed, outs):
    per_device = summed.shape[1]
    parts = VALUE_SIZE // KEY_SIZE
    t = 0
    for query, value in outs:
        for lane in range(0, query.shape[1], LANES):
            count = min(LANES, query.shape[1] - lane)
            got = [summed[(t + i) // per_device, (t + i) % per_device] for i in range(1 + parts)]
            query[:, lane : lane + count] = got[0][:, :count]
            value[:, lane : lane + count] = jnp.concatenate(got[1:], axis=0)[:, :count]
            t += 1 + parts


def fill_table(table_ref, padded, turn):
    padded[...] = jnp.zeros_like(padded)
    padded[: padded.shape[0] - 1, :] = (
        table_ref[...].astype(F32).T.astype(BF16) if turn else table_ref[...]
    )


def layer_kernel(
    sizes,
    x_ref, rq_in, rv_in, qk_ref, g_ref, cq_in, cv_in,
    gx_ref, gqk_ref, tq_ref, tv_ref, ctq_ref, ctv_ref,
    rq_ref, rv_ref, cq_ref, cv_ref, qk_cells, g_cells, gqk_cells, pc_ref,
    x_lines, p_ref, w_ref, out_lines, values_in, values, grads, grads_out, d_lines, gx_lines,
    row_query, row_value, column_query, column_value, packed, got, part, got_part, summed,
    x_send, x_recv, b_send, b_recv, c_send, c_recv, g_send, g_recv, t_send, t_recv,
    u_send, u_recv, s_send, s_recv,
):
    ha_size, wa_size = sizes
    count = ha_size * wa_size
    ha, wa = lax.axis_index("ha"), lax.axis_index("wa")
    me = ha * wa_size + wa
    to_id = lambda i: peer_id(i, sizes)
    to_wa = lambda i: {"ha": ha, "wa": i}
    lines = x_lines.shape[1]
    height = values.shape[0]
    columns = qk_ref.shape[1]
    greet(me, count, to_id)

    def swap_x(n, begin):
        return swap_all(
            wa,
            wa_size,
            to_wa,
            lambda i: x_ref.at[i * lines + n],
            lambda i: x_lines.at[i, n],
            x_send.at[n],
            x_recv.at[n],
            begin,
        )

    def swap_b(n, begin):
        return swap_all(
            me,
            count,
            to_id,
            lambda i: out_lines.at[i, n],
            lambda i: values_in.at[i * lines + n],
            b_send.at[n],
            b_recv.at[n],
            begin,
        )

    def each_line(step):
        def body(n, carry):
            step(n)
            return carry

        lax.fori_loop(0, lines, body, 0)

    each_line(lambda n: swap_x(n, True))
    x_lines[wa] = x_ref[pl.ds(wa * lines, lines)]
    fill_table(rq_in, rq_ref, True)
    fill_table(rv_in, rv_ref, False)
    fill_table(cq_in, cq_ref, True)
    fill_table(cv_in, cv_ref, False)
    qk_cells[:, :columns] = qk_ref[...].astype(F32)
    g_cells[:, :columns] = g_ref[...].astype(F32)

    def swap_c(begin):
        return swap_all(
            me,
            count,
            to_id,
            lambda i: grads_out.at[pl.ds(i * lines, lines)],
            lambda i: d_lines.at[i],
            c_send,
            c_recv,
            begin,
        )

    def swap_line(n, begin):
        return swap_all(
            wa,
            wa_size,
            to_wa,
            lambda i: gx_lines.at[i, n],
            lambda i: gx_ref.at[i * lines + n],
            g_send.at[n],
            g_recv.at[n],
            begin,
        )

    def send_b(n):
        swap_b(n, True)
        values_in[me * lines + n] = out_lines[me, n]

    def send(n):
        swap_line(n, True)
        gx_ref[wa * lines + n] = gx_lines[wa, n]

    cells = lambda ref: ref.reshape(height * SUBLANES, VALUE_WIDTH)
    columns_step = lambda first: column_pass(
        first,
        columns,
        cells(qk_cells),
        cells(values),
        cells(g_cells),
        cq_ref,
        cv_ref,
        cells(gqk_cells),
        cells(grads),
        column_query,
        column_value,
        pc_ref,
    )
    columns_step(True)
    grads_out[...] = grads[...].astype(BF16)
    swap_c(True)
    d_lines[me] = grads_out[pl.ds(me * lines, lines)]
    row_forward(
        x_lines, rq_ref, rv_ref, out_lines, p_ref, w_ref, lambda n: swap_x(n, False)(), send_b
    )
    swap_c(False)()
    row_backward(
        x_lines, d_lines, p_ref, w_ref, rq_ref, rv_ref, gx_lines, row_query, row_value, send
    )
    each_line(lambda n: swap_b(n, False)())
    values[...] = values_in[...].astype(F32)
    columns_step(False)
    pack_tables([(row_query, row_value), (column_query, column_value)], packed)
    to_ha = lambda i: {"ha": i, "wa": wa}
    finish = swap_all(
        ha, ha_size, to_ha, lambda i: packed.at[i], lambda i: got.at[i], t_send, t_recv
    )
    got[ha] = packed[ha]
    gqk_ref[...] = gqk_cells[:, :columns].astype(BF16)
    finish()
    total = got[0].astype(F32)
    for i in range(1, ha_size):
        total = total + got[i].astype(F32)
    part[...] = total
    finish = swap_all(
        wa, wa_size, to_wa, lambda i: part.at[i], lambda i: got_part.at[i], u_send, u_recv
    )
    got_part[wa] = part[wa]
    finish()
    total = got_part[0]
    for i in range(1, wa_size):
        total = total + got_part[i]
    summed[ha] = total
    finish = swap_all(
        ha,
        ha_size,
        to_ha,
        lambda i: summed.at[ha],
        lambda i: summed.at[i],
        s_send,
        s_recv,
    )
    finish()
    unpack_tables(summed, [(tq_ref, tv_ref), (ctq_ref, ctv_ref)])

    each_line(lambda n: swap_line(n, False)())


def layer(x, rq, rv, qk, g, cq, cv):
    sizes = (lax.axis_size("ha"), lax.axis_size("wa"))
    ha_size, wa_size = sizes
    count = ha_size * wa_size
    tile_rows, tile, channels = x.shape
    lines, length = tile_rows // wa_size, tile * wa_size
    height, columns, _ = qk.shape
    rows = QUERY_WIDTH // wa_size
    tiles = (1 + VALUE_SIZE // KEY_SIZE) * 2 * (length + height) // LANES
    per_device = -(-tiles // ha_size)
    operands = (x, rq, rv, qk, g, cq, cv)
    out_shapes = [
        (x.shape, BF16),
        (qk.shape, BF16),
        ((rows, 2 * length - 1), F32),
        ((VALUE_WIDTH // wa_size, 2 * length - 1), F32),
        ((rows, 2 * height - 1), F32),
        ((VALUE_WIDTH // wa_size, 2 * height - 1), F32),
    ]
    scratch = [
        ((2 * length, QUERY_WIDTH), BF16),
        ((2 * length, VALUE_WIDTH), BF16),
        ((2 * height, QUERY_WIDTH), BF16),
        ((2 * height, VALUE_WIDTH), BF16),
        ((height, SUBLANES, VALUE_WIDTH), F32),
        ((height, SUBLANES, VALUE_WIDTH), F32),
        ((height, SUBLANES, VALUE_WIDTH), F32),
        ((columns, HEAD_COUNT * height, height), F32),
        ((wa_size, lines, tile, channels), BF16),
        ((lines, HEAD_COUNT, length, length), F32),
        ((lines, HEAD_COUNT, length, 3 * length), BF16),
        ((count, lines, SUBLANES, VALUE_WIDTH), BF16),
        ((height, SUBLANES, VALUE_WIDTH), BF16),
        ((height, SUBLANES, VALUE_WIDTH), F32),
        ((height, SUBLANES, VALUE_WIDTH), F32),
        ((height, SUBLANES, VALUE_WIDTH), BF16),
        ((count, lines, SUBLANES, VALUE_WIDTH), BF16),
        ((wa_size, lines, tile, channels), BF16),
        ((QUERY_WIDTH, 2 * length), F32),
        ((VALUE_WIDTH, 2 * length), F32),
        ((QUERY_WIDTH, 2 * height), F32),
        ((VALUE_WIDTH, 2 * height), F32),
        ((ha_size, wa_size, per_device, rows, LANES), BF16),
        ((ha_size, wa_size, per_device, rows, LANES), BF16),
        ((wa_size, per_device, rows, LANES), F32),
        ((wa_size, per_device, rows, LANES), F32),
        ((ha_size, per_device, rows, LANES), F32),
    ]
    semaphores = [
        (lines, wa_size),
        (lines, count),
        (count,),
        (lines, wa_size),
        (ha_size,),
        (wa_size,),
        (ha_size,),
    ]
    return pl.pallas_call(
        functools.partial(layer_kernel, sizes),
        name="layer",
        out_shape=[jax.ShapeDtypeStruct(s, t) for s, t in out_shapes],
        in_specs=[pl.BlockSpec(memory_space=pltpu.VMEM)] * len(operands),
        out_specs=[pl.BlockSpec(memory_space=pltpu.VMEM)] * len(out_shapes),
        scratch_shapes=[pltpu.VMEM(s, t) for s, t in scratch]
        + [pltpu.SemaphoreType.DMA(s) for s in semaphores for _ in range(2)],
        compiler_params=pltpu.CompilerParams(
            collective_id=0, has_side_effects=True, vmem_limit_bytes=56 * 1024 * 1024
        ),
    )(*operands)


def on_device(
    row_features,
    row_table_query,
    row_table_value,
    column_query_key,
    column_table_query,
    column_table_value,
    output_cotangent,
):
    outs = layer(
        row_features,
        row_table_query.T,
        row_table_value,
        column_query_key,
        output_cotangent,
        column_table_query.T,
        column_table_value,
    )
    return (outs[0], outs[1], *(t.T for t in outs[2:]))


def solution(mesh):
    placed = (
        P("ha", "wa", None),
        P(),
        P(),
        P(None, ("ha", "wa"), None),
        P(),
        P(),
        P(None, ("ha", "wa"), None),
    )
    return jax.shard_map(
        on_device,
        mesh=mesh,
        in_specs=placed,
        out_specs=(
            P("ha", "wa", None),
            P(None, ("ha", "wa"), None),
            P(None, "wa"),
            P(None, "wa"),
            P(None, "wa"),
            P(None, "wa"),
        ),
        check_vma=False,
    )
```
